256 devices in a mesh: orb: 64 (over x, z_lo, y, core), pan: 4 (over z_hi).
Axes of the slice: x: 4, y: 4, z: 8 (z_hi: 4, z_lo: 2; z = z_hi * 2 + z_lo), core: 2. Of those that a mesh axis runs over, the one named last changes fastest.
Arguments:
- orbitals: float32 [1024, 110592], P(('orb', 'pan')), may hold values from -6 to 6
- potential: float32 [110592], replicated, may hold values from -1 to 2
- magic_taps: float32 [16], replicated, may hold values from -4 to 4
- kinetic_taps: float32 [29], replicated, may hold values from -3 to 3
Outputs:
- gradient: float32 [1024, 110592], P(('orb', 'pan'))
The draws below stay inside these ranges and needn't reach their ends.
All inputs are finite; a program needn't handle non-finite values.
Results may differ from the reference program's by a relative error of at most 0.00013.
Values sent between devices are 32-bit elements; how exact they have to be, the bound alone decides.
No kernel may reach another device: no remote copies, remote signals or barrier semaphores. Data moves between devices by JAX's collectives and lax.ppermute only.
A program may use at most 128 MiB of HBM per device.

```python
import jax
import jax.numpy as jnp
from jax import lax

G = 48
MAGIC_TAPS = 16
KIN_TAPS = 29
NC = 110592
NORB = 1024
N_PAN = 4


def level_of(stream_key, shape, shards, least, high):
    factor_of, own = 1.0, jax.random.fold_in(stream_key, 6)
    for position, shards_of in shards:
        draws = jnp.exp(jax.random.uniform(jax.random.fold_in(own, position), (shards_of,), jnp.float32, least / len(shards), high / len(shards)))
        factor_of = factor_of * jnp.repeat(draws, shape[position] // shards_of).reshape([-1 if axis == position else 1 for axis in range(len(shape))])
    return factor_of


def scatter_about(key, dims, spread, limit, shards=(), kind=jnp.bfloat16):
    drawn = jax.random.normal(key, dims, jnp.float32) * spread
    if len(shards) > 0:
        drawn = level_of(key, dims, shards, -0.22, 0.18) * drawn
    return jnp.clip(drawn, min=-limit, max=limit).astype(kind)


def setup_inputs(seed: int = 0) -> dict:
    streams_of = jax.random.split(jax.random.key(seed), 5)
    orbitals = scatter_about(streams_of[0], (NORB, NC), 1.0, 6.0, ((0, 256),), jnp.float32)
    potential = jnp.clip(jax.random.uniform(streams_of[1], (NC,), jnp.float32, -1.0, 2.0), -1.0, 2.0)
    magic_taps = scatter_about(streams_of[2], (MAGIC_TAPS,), 0.25, 4.0, (), jnp.float32)
    kinetic_taps = scatter_about(streams_of[3], (KIN_TAPS,), 0.2, 3.0, (), jnp.float32)
    return dict(orbitals=orbitals, potential=potential, magic_taps=magic_taps, kinetic_taps=kinetic_taps)


def filter_matrix(tap_values, extent):
    tap_count = tap_values.shape[0]
    centre = (tap_count - 1) // 2
    tap_ids = lax.broadcasted_iota(jnp.int32, (tap_count, extent, extent), 0)
    row_ids = lax.broadcasted_iota(jnp.int32, (tap_count, extent, extent), 1)
    col_ids = lax.broadcasted_iota(jnp.int32, (tap_count, extent, extent), 2)
    offset = (col_ids - row_ids - (tap_ids - centre)) % extent
    return jnp.sum(jnp.where(offset == 0, tap_values[:, None, None], jnp.float32(0.0)), axis=0)


def along(matrix, volume, which_axis):
    patterns = {1: "ab,nbcd->nacd", 2: "ab,ncbd->ncad", 3: "ab,ncdb->ncda"}
    return jnp.einsum(patterns[which_axis], matrix, volume, precision=lax.Precision.HIGHEST)


def hamiltonian(block, potential, magic_matrix, kinetic_matrix):
    count_here = block.shape[0]
    volume = block.reshape(count_here, G, G, G)
    smooth = volume
    for which_axis in (1, 2, 3):
        smooth = along(magic_matrix, smooth, which_axis)
    smooth = smooth * potential.reshape(1, G, G, G)
    for which_axis in (1, 2, 3):
        smooth = along(magic_matrix.T, smooth, which_axis)
    kinetic_part = along(kinetic_matrix, volume, 1) + along(kinetic_matrix, volume, 2) + along(kinetic_matrix, volume, 3)
    return (smooth + kinetic_part).reshape(count_here, G * G * G)


def reference(orbitals, potential, magic_taps, kinetic_taps):
    magic_matrix = filter_matrix(magic_taps, G)
    kinetic_matrix = filter_matrix(kinetic_taps, G)
    blocks = orbitals.reshape(N_PAN, -1, NC)
    hpsi = lax.map(lambda block: hamiltonian(block, potential, magic_matrix, kinetic_matrix), blocks).reshape(NORB, NC)
    margin = jnp.einsum("jc,ic->ji", orbitals, hpsi, precision=lax.Precision.HIGHEST) * (1.0 / NC)
    rotated = jnp.einsum("ji,jc->ic", margin, orbitals, precision=lax.Precision.HIGHEST)
    return hpsi - rotated
```

```python
import jax
import jax.numpy as jnp
from jax import lax
from jax.sharding import Mesh, PartitionSpec as P

G = 48
NC = 110592
SPLIT = (4, 2, 4, 2, 4)
NAMES = ("x", "zl", "y", "core", "zh")
COEF = ("y", "zl", "zh")
PANEL = ("x", "core")
NSPLIT = 32
HIGH = lax.Precision.HIGH


def filter_matrix(tap_values, extent):
    tap_count = tap_values.shape[0]
    centre = (tap_count - 1) // 2
    tap_ids = lax.broadcasted_iota(jnp.int32, (tap_count, extent, extent), 0)
    row_ids = lax.broadcasted_iota(jnp.int32, (tap_count, extent, extent), 1)
    col_ids = lax.broadcasted_iota(jnp.int32, (tap_count, extent, extent), 2)
    offset = (col_ids - row_ids - (tap_ids - centre)) % extent
    return jnp.sum(jnp.where(offset == 0, tap_values[:, None, None], jnp.float32(0.0)), axis=0)


def along(matrix, volume, which_axis):
    patterns = {1: "ab,nbcd->nacd", 2: "ab,ncbd->ncad", 3: "ab,ncdb->ncda"}
    return jnp.einsum(patterns[which_axis], matrix, volume, precision=HIGH)


def hamiltonian(block, potential, magic_matrix, kinetic_matrix):
    count_here = block.shape[0]
    volume = block.reshape(count_here, G, G, G)
    smooth = volume
    for which_axis in (1, 2, 3):
        smooth = along(magic_matrix, smooth, which_axis)
    smooth = smooth * potential.reshape(1, G, G, G)
    for which_axis in (1, 2, 3):
        smooth = along(magic_matrix.T, smooth, which_axis)
    kinetic_part = (
        along(kinetic_matrix, volume, 1)
        + along(kinetic_matrix, volume, 2)
        + along(kinetic_matrix, volume, 3)
    )
    return (smooth + kinetic_part).reshape(count_here, G * G * G)


def to_cols(block):
    return lax.all_to_all(block, COEF, split_axis=1, concat_axis=0, tiled=True)


def shards(orbitals, potential, magic_taps, kinetic_taps):
    magic_matrix = filter_matrix(magic_taps, G)
    kinetic_matrix = filter_matrix(kinetic_taps, G)
    psi_cols = to_cols(orbitals)
    psi_every = lax.all_gather(psi_cols, PANEL, axis=0, tiled=True)
    hpsi = hamiltonian(orbitals, potential, magic_matrix, kinetic_matrix)
    hpsi_cols = to_cols(hpsi)
    part = jnp.einsum("jc,ic->ji", psi_every, hpsi_cols, precision=HIGH) * (1.0 / NC)
    rows = part.shape[0] // NSPLIT
    pieces = lax.all_to_all(
        part.reshape(NSPLIT, rows, -1), COEF, split_axis=0, concat_axis=0, tiled=True
    )
    mine = jnp.sum(pieces, axis=0)
    margin = lax.all_to_all(
        jnp.broadcast_to(mine[None], pieces.shape), COEF, split_axis=0, concat_axis=0, tiled=True
    ).reshape(part.shape)
    grad_cols = hpsi_cols - jnp.einsum("ji,jc->ic", margin, psi_every, precision=HIGH)
    return lax.all_to_all(grad_cols, COEF, split_axis=0, concat_axis=1, tiled=True)


def solution(mesh):
    fine = Mesh(mesh.devices.reshape(SPLIT), NAMES)
    placed = (P(NAMES, None), P(), P(), P())
    return jax.shard_map(
        shards, mesh=fine, in_specs=placed, out_specs=P(NAMES, None), check_vma=False
    )
```

```python
import jax
import jax.numpy as jnp
from jax import lax
from jax.experimental import pallas as pl
from jax.experimental.pallas import tpu as pltpu
from jax.sharding import Mesh, PartitionSpec as P

G = 48
NC = 110592
SPLIT = (4, 2, 4, 2, 4)
NAMES = ("x", "zl", "y", "core", "zh")
COEF = ("y", "zl", "zh")
PANEL = ("x", "core")
NSPLIT = 32
HIGH = lax.Precision.HIGH
PLANE = G * G
BLK = 16 * G
F32 = jnp.float32
BF16 = jnp.bfloat16


def split_bf16(value):
    high = value.astype(BF16)
    return high, (value - high.astype(F32)).astype(BF16)


def pick_taps(taps_ref, count, offset):
    out = jnp.zeros(offset.shape, F32)
    for k in range(count):
        out = jnp.where(offset == k, taps_ref[k], out)
    return out


def wrap(offset):
    return jnp.where(offset < 0, offset + G, jnp.where(offset >= G, offset - G, offset))


def ints(shape, dim):
    return lax.broadcasted_iota(jnp.int32, shape, dim)


def div_g(value):
    return (value * 1366) >> 16


def x_matrix(taps_ref, count, rows, transposed):
    shape = (rows, rows)
    r, c = ints(shape, 0), ints(shape, 1)
    gap = (r >> 2) - (c >> 2) if transposed else (c >> 2) - (r >> 2)
    offset = wrap(gap + (count - 1) // 2)
    return jnp.where((r & 3) == (c & 3), pick_taps(taps_ref, count, offset), 0.0)


def z_table(taps_ref, count, transposed):
    shape = (G, BLK)
    lane = ints(shape, 1)
    z_out = lane - G * div_g(lane)
    z_in = ints(shape, 0)
    gap = z_out - z_in if transposed else z_in - z_out
    return pick_taps(taps_ref, count, wrap(gap + (count - 1) // 2))


def y_table(taps_ref, count, reach, transposed):
    shape = (16 + 2 * reach, BLK)
    gap = ints(shape, 0) - reach - div_g(ints(shape, 1))
    if transposed:
        gap = -gap
    return pick_taps(taps_ref, count, gap + (count - 1) // 2)


def h_kernel(magic_ref, kinetic_ref, psi_ref, pot_ref, out_ref,
             s, t, zt, zt2, yt, w_hi, w_lo, lhs, prod, pad, xm):
    rows = s.shape[0]
    n_magic, n_kin = magic_ref.shape[0], kinetic_ref.shape[0]

    def fill_weights(depth, with_identity):
        def body(j, carry):
            value = zt[...] * yt[pl.ds(j, 1), :]
            if with_identity:
                lane = ints((1, BLK), 1)
                same = jnp.where(div_g(lane) == j - 16, 1.0, 0.0).astype(F32)
                value = value + zt2[...] * same
            high, low = split_bf16(value)
            at = pl.multiple_of(j * G, G)
            w_hi[pl.ds(at, G), :] = high
            w_lo[pl.ds(at, G), :] = low
            return carry
        lax.fori_loop(0, depth, body, 0)

    def fill_lhs(source, reach):
        edge = reach * G
        width = (16 + 2 * reach) * G
        for part in range(2):
            pad[:, 0:PLANE] = split_bf16(source[...])[part]
            pad[:, PLANE:2 * PLANE] = pad[:, 0:PLANE]
            for n in range(3):
                start = (BLK * n - edge) % PLANE
                lhs[pl.ds((3 * part + n) * rows, rows), 0:width] = pad[:, start:start + width]

    def kron(width, accumulate, target):
        def body(nt, carry):
            at = pl.multiple_of(nt * 256, 256)
            cols = pl.ds(at, 256)
            prod[...] = jnp.dot(lhs[:, 0:width], w_hi[0:width, cols], preferred_element_type=F32)
            low = jnp.dot(lhs[0:3 * rows, 0:width], w_lo[0:width, cols], preferred_element_type=F32)
            for n in range(3):
                value = (prod[n * rows:(n + 1) * rows, :] + prod[(3 + n) * rows:(4 + n) * rows, :]
                         + low[n * rows:(n + 1) * rows, :])
                place = pl.ds(pl.multiple_of(BLK * n + nt * 256, 256), 256)
                if accumulate:
                    value = value + target[:, place]
                target[:, place] = value
            return carry
        lax.fori_loop(0, 3, body, 0)

    def along_x(matrix, source, finish):
        high, low = split_bf16(matrix)
        xm[0:rows, :] = high
        xm[rows:, :] = low

        def body(nt, carry):
            cols = pl.ds(pl.multiple_of(nt * 256, 256), 256)
            b_hi, b_lo = split_bf16(source[:, cols])
            both = jnp.dot(xm[...], b_hi, preferred_element_type=F32)
            low = jnp.dot(xm[0:rows, :], b_lo, preferred_element_type=F32)
            finish(cols, both[0:rows] + both[rows:] + low)
            return carry
        lax.fori_loop(0, PLANE // 256, body, 0)

    for x in range(G):
        s[4 * x:4 * x + 4, :] = psi_ref[:, x * PLANE:(x + 1) * PLANE]

    zt[...] = z_table(magic_ref, n_magic, False)
    yt[0:32, :] = y_table(magic_ref, n_magic, 8, False)
    fill_weights(32, False)
    fill_lhs(s, 8)
    kron(2 * BLK, False, t)

    def magic_and_potential(cols, value):
        pot = pot_ref[:, cols]
        t[:, cols] = value * jnp.broadcast_to(pot[:, None, :], (G, 4, 256)).reshape(rows, 256)

    along_x(x_matrix(magic_ref, n_magic, rows, False), t, magic_and_potential)

    def keep(cols, value):
        t[:, cols] = value

    along_x(x_matrix(magic_ref, n_magic, rows, True), t, keep)

    zt[...] = z_table(magic_ref, n_magic, True)
    yt[0:32, :] = y_table(magic_ref, n_magic, 8, True)
    fill_weights(32, False)
    fill_lhs(t, 8)

    def start_sum(cols, value):
        t[:, cols] = value

    along_x(x_matrix(kinetic_ref, n_kin, rows, False), s, start_sum)
    kron(2 * BLK, True, t)

    shape = (G, BLK)
    lane = ints(shape, 1)
    zt[...] = jnp.where(lane - G * div_g(lane) == ints(shape, 0), 1.0, 0.0).astype(F32)
    zt2[...] = z_table(kinetic_ref, n_kin, False)
    yt[...] = y_table(kinetic_ref, n_kin, 16, False)
    fill_weights(48, True)
    fill_lhs(s, 16)
    kron(3 * BLK, True, t)

    for x in range(G):
        out_ref[:, x * PLANE:(x + 1) * PLANE] = t[4 * x:4 * x + 4, :]


def hamiltonian(orbitals, potential, magic_taps, kinetic_taps):
    count = orbitals.shape[0]
    rows = count * G
    vmem = pl.BlockSpec(memory_space=pltpu.VMEM)
    smem = pl.BlockSpec(memory_space=pltpu.SMEM)
    return pl.pallas_call(
        h_kernel,
        out_shape=jax.ShapeDtypeStruct(orbitals.shape, F32),
        in_specs=[smem, smem, vmem, vmem],
        out_specs=vmem,
        scratch_shapes=[
            pltpu.VMEM((rows, PLANE), F32),
            pltpu.VMEM((rows, PLANE), F32),
            pltpu.VMEM((G, BLK), F32),
            pltpu.VMEM((G, BLK), F32),
            pltpu.VMEM((G, BLK), F32),
            pltpu.VMEM((PLANE, BLK), BF16),
            pltpu.VMEM((PLANE, BLK), BF16),
            pltpu.VMEM((6 * rows, PLANE), BF16),
            pltpu.VMEM((6 * rows, 256), F32),
            pltpu.VMEM((rows, 2 * PLANE), BF16),
            pltpu.VMEM((2 * rows, rows), BF16),
        ],
        compiler_params=pltpu.CompilerParams(vmem_limit_bytes=48 * 1024 * 1024),
        name="hamiltonian",
    )(magic_taps, kinetic_taps, orbitals, potential.reshape(G, PLANE))


def to_cols(block):
    return lax.all_to_all(block, COEF, split_axis=1, concat_axis=0, tiled=True)


def shards(orbitals, potential, magic_taps, kinetic_taps):
    psi_cols = to_cols(orbitals)
    psi_every = lax.all_gather(psi_cols, PANEL, axis=0, tiled=True)
    hpsi = hamiltonian(orbitals, potential, magic_taps, kinetic_taps)
    hpsi_cols = to_cols(hpsi)
    part = jnp.einsum("jc,ic->ji", psi_every, hpsi_cols, precision=HIGH) * (1.0 / NC)
    rows = part.shape[0] // NSPLIT
    pieces = lax.all_to_all(
        part.reshape(NSPLIT, rows, -1), COEF, split_axis=0, concat_axis=0, tiled=True
    )
    mine = jnp.sum(pieces, axis=0)
    margin = lax.all_to_all(
        jnp.broadcast_to(mine[None], pieces.shape), COEF, split_axis=0, concat_axis=0, tiled=True
    ).reshape(part.shape)
    grad_cols = hpsi_cols - jnp.einsum("ji,jc->ic", margin, psi_every, precision=HIGH)
    return lax.all_to_all(grad_cols, COEF, split_axis=0, concat_axis=1, tiled=True)


def solution(mesh):
    fine = Mesh(mesh.devices.reshape(SPLIT), NAMES)
    placed = (P(NAMES, None), P(), P(), P())
    return jax.shard_map(
        shards, mesh=fine, in_specs=placed, out_specs=P(NAMES, None), check_vma=False
    )
```

```python
import jax
import jax.numpy as jnp
from jax import lax
from jax.experimental import pallas as pl
from jax.experimental.pallas import tpu as pltpu
from jax.sharding import Mesh, PartitionSpec as P

G = 48
NC = 110592
SPLIT = (4, 2, 4, 2, 4)
NAMES = ("x", "zl", "y", "core", "zh")
COEF = ("y", "zl", "zh")
PANEL = ("x", "core")
NSPLIT = 32
FIRST = 14 * 128
HIGH = lax.Precision.HIGH
PLANE = G * G
BLK = 16 * G
F32 = jnp.float32
BF16 = jnp.bfloat16


def split_bf16(value):
    high = value.astype(BF16)
    return high, (value - high.astype(F32)).astype(BF16)


def pick_taps(taps_ref, count, offset):
    out = jnp.zeros(offset.shape, F32)
    for k in range(count):
        out = jnp.where(offset == k, taps_ref[k], out)
    return out


def wrap(offset):
    return jnp.where(offset < 0, offset + G, jnp.where(offset >= G, offset - G, offset))


def ints(shape, dim):
    return lax.broadcasted_iota(jnp.int32, shape, dim)


def div_g(value):
    return (value * 1366) >> 16


def x_matrix(taps_ref, count, rows, transposed):
    shape = (rows, rows)
    r, c = ints(shape, 0), ints(shape, 1)
    gap = (r >> 2) - (c >> 2) if transposed else (c >> 2) - (r >> 2)
    offset = wrap(gap + (count - 1) // 2)
    return jnp.where((r & 3) == (c & 3), pick_taps(taps_ref, count, offset), 0.0)


def z_table(taps_ref, count, transposed):
    shape = (G, BLK)
    lane = ints(shape, 1)
    z_out = lane - G * div_g(lane)
    z_in = ints(shape, 0)
    gap = z_out - z_in if transposed else z_in - z_out
    return pick_taps(taps_ref, count, wrap(gap + (count - 1) // 2))


def y_table(taps_ref, count, reach, transposed):
    shape = (16 + 2 * reach, BLK)
    gap = ints(shape, 0) - reach - div_g(ints(shape, 1))
    if transposed:
        gap = -gap
    return pick_taps(taps_ref, count, gap + (count - 1) // 2)


def h_kernel(magic_ref, kinetic_ref, psi_ref, pot_ref, out_ref,
             s, t, zt, zt2, yt, w_hi, w_lo, lhs, prod, pad, xm):
    rows = s.shape[0]
    n_magic, n_kin = magic_ref.shape[0], kinetic_ref.shape[0]

    def fill_weights(depth, with_identity):
        def body(j, carry):
            value = zt[...] * yt[pl.ds(j, 1), :]
            if with_identity:
                lane = ints((1, BLK), 1)
                same = jnp.where(div_g(lane) == j - 16, 1.0, 0.0).astype(F32)
                value = value + zt2[...] * same
            high, low = split_bf16(value)
            at = pl.multiple_of(j * G, G)
            w_hi[pl.ds(at, G), :] = high
            w_lo[pl.ds(at, G), :] = low
            return carry
        lax.fori_loop(0, depth, body, 0)

    def fill_lhs(source, reach):
        edge = reach * G
        width = (16 + 2 * reach) * G
        for part in range(2):
            pad[:, 0:PLANE] = split_bf16(source[...])[part]
            pad[:, PLANE:2 * PLANE] = pad[:, 0:PLANE]
            for n in range(3):
                start = (BLK * n - edge) % PLANE
                lhs[pl.ds((3 * part + n) * rows, rows), 0:width] = pad[:, start:start + width]

    def kron(width, accumulate, target):
        def body(nt, carry):
            at = pl.multiple_of(nt * 256, 256)
            cols = pl.ds(at, 256)
            prod[...] = jnp.dot(lhs[:, 0:width], w_hi[0:width, cols], preferred_element_type=F32)
            low = jnp.dot(lhs[0:3 * rows, 0:width], w_lo[0:width, cols], preferred_element_type=F32)
            for n in range(3):
                value = (prod[n * rows:(n + 1) * rows, :] + prod[(3 + n) * rows:(4 + n) * rows, :]
                         + low[n * rows:(n + 1) * rows, :])
                place = pl.ds(pl.multiple_of(BLK * n + nt * 256, 256), 256)
                if accumulate:
                    value = value + target[:, place]
                target[:, place] = value
            return carry
        lax.fori_loop(0, 3, body, 0)

    def along_x(matrix, source, finish):
        high, low = split_bf16(matrix)
        xm[0:rows, :] = high
        xm[rows:, :] = low

        def body(nt, carry):
            cols = pl.ds(pl.multiple_of(nt * 256, 256), 256)
            b_hi, b_lo = split_bf16(source[:, cols])
            both = jnp.dot(xm[...], b_hi, preferred_element_type=F32)
            low = jnp.dot(xm[0:rows, :], b_lo, preferred_element_type=F32)
            finish(cols, both[0:rows] + both[rows:] + low)
            return carry
        lax.fori_loop(0, PLANE // 256, body, 0)

    for x in range(G):
        s[4 * x:4 * x + 4, :] = psi_ref[:, x * PLANE:(x + 1) * PLANE]

    zt[...] = z_table(magic_ref, n_magic, False)
    yt[0:32, :] = y_table(magic_ref, n_magic, 8, False)
    fill_weights(32, False)
    fill_lhs(s, 8)
    kron(2 * BLK, False, t)

    def magic_and_potential(cols, value):
        pot = pot_ref[:, cols]
        t[:, cols] = value * jnp.broadcast_to(pot[:, None, :], (G, 4, 256)).reshape(rows, 256)

    along_x(x_matrix(magic_ref, n_magic, rows, False), t, magic_and_potential)

    def keep(cols, value):
        t[:, cols] = value

    along_x(x_matrix(magic_ref, n_magic, rows, True), t, keep)

    zt[...] = z_table(magic_ref, n_magic, True)
    yt[0:32, :] = y_table(magic_ref, n_magic, 8, True)
    fill_weights(32, False)
    fill_lhs(t, 8)

    def start_sum(cols, value):
        t[:, cols] = value

    along_x(x_matrix(kinetic_ref, n_kin, rows, False), s, start_sum)
    kron(2 * BLK, True, t)

    shape = (G, BLK)
    lane = ints(shape, 1)
    zt[...] = jnp.where(lane - G * div_g(lane) == ints(shape, 0), 1.0, 0.0).astype(F32)
    zt2[...] = z_table(kinetic_ref, n_kin, False)
    yt[...] = y_table(kinetic_ref, n_kin, 16, False)
    fill_weights(48, True)
    fill_lhs(s, 16)
    kron(3 * BLK, True, t)

    for x in range(G):
        out_ref[:, x * PLANE:(x + 1) * PLANE] = t[4 * x:4 * x + 4, :]


def hamiltonian(orbitals, potential, magic_taps, kinetic_taps):
    count = orbitals.shape[0]
    rows = count * G
    vmem = pl.BlockSpec(memory_space=pltpu.VMEM)
    smem = pl.BlockSpec(memory_space=pltpu.SMEM)
    return pl.pallas_call(
        h_kernel,
        out_shape=jax.ShapeDtypeStruct(orbitals.shape, F32),
        in_specs=[smem, smem, vmem, vmem],
        out_specs=vmem,
        scratch_shapes=[
            pltpu.VMEM((rows, PLANE), F32),
            pltpu.VMEM((rows, PLANE), F32),
            pltpu.VMEM((G, BLK), F32),
            pltpu.VMEM((G, BLK), F32),
            pltpu.VMEM((G, BLK), F32),
            pltpu.VMEM((PLANE, BLK), BF16),
            pltpu.VMEM((PLANE, BLK), BF16),
            pltpu.VMEM((6 * rows, PLANE), BF16),
            pltpu.VMEM((6 * rows, 256), F32),
            pltpu.VMEM((rows, 2 * PLANE), BF16),
            pltpu.VMEM((2 * rows, rows), BF16),
        ],
        compiler_params=pltpu.CompilerParams(vmem_limit_bytes=48 * 1024 * 1024),
        cost_estimate=pl.CostEstimate(
            flops=24_000_000_000, transcendentals=0, bytes_accessed=12 * orbitals.size
        ),
        name="hamiltonian",
    )(magic_taps, kinetic_taps, orbitals, potential.reshape(G, PLANE))


def to_cols(block):
    return lax.all_to_all(block, COEF, split_axis=1, concat_axis=0, tiled=True).reshape(
        NSPLIT * block.shape[0], -1
    )


def shards(orbitals, potential, magic_taps, kinetic_taps):
    pieces = orbitals.reshape(orbitals.shape[0], NSPLIT, -1)
    first, second = pieces[:, :, :FIRST], pieces[:, :, FIRST:]
    cols_1 = to_cols(first)
    hpsi = hamiltonian(orbitals, potential, magic_taps, kinetic_taps)
    cols_1, hpsi, second = lax.optimization_barrier((cols_1, hpsi, second))
    every_1 = lax.all_gather(cols_1, PANEL, axis=0, tiled=True)
    cols_2 = to_cols(second)
    cols_2, hpsi = lax.optimization_barrier((cols_2, hpsi))
    every_2 = lax.all_gather(cols_2, PANEL, axis=0, tiled=True)
    hpsi_cols = to_cols(hpsi.reshape(pieces.shape))
    parts = ((every_1, hpsi_cols[:, :FIRST]), (every_2, hpsi_cols[:, FIRST:]))
    part = sum(jnp.einsum("jc,ic->ji", psi, own, precision=HIGH) for psi, own in parts) * (1.0 / NC)
    rows = part.shape[0] // NSPLIT
    terms = lax.all_to_all(
        part.reshape(NSPLIT, rows, -1), COEF, split_axis=0, concat_axis=0, tiled=True
    )
    mine = jnp.sum(terms, axis=0)
    margin = lax.all_to_all(
        jnp.broadcast_to(mine[None], terms.shape), COEF, split_axis=0, concat_axis=0, tiled=True
    ).reshape(part.shape)
    grad_cols = jnp.concatenate(
        [own - jnp.einsum("ji,jc->ic", margin, psi, precision=HIGH) for psi, own in parts], axis=1
    )
    return lax.all_to_all(grad_cols, COEF, split_axis=0, concat_axis=1, tiled=True)


def solution(mesh):
    fine = Mesh(mesh.devices.reshape(SPLIT), NAMES)
    placed = (P(NAMES, None), P(), P(), P())
    return jax.shard_map(
        shards, mesh=fine, in_specs=placed, out_specs=P(NAMES, None), check_vma=False
    )
```

```python
import jax
import jax.numpy as jnp
from jax import lax
from jax.experimental import pallas as pl
from jax.experimental.pallas import tpu as pltpu
from jax.sharding import Mesh, PartitionSpec as P

G = 48
NC = 110592
SPLIT = (4, 2, 4, 2, 4)
NAMES = ("x", "zl", "y", "core", "zh")
COEF = ("y", "zl", "zh")
NSPLIT = 32
HIGH = lax.Precision.HIGH
PLANE = G * G
BLK = 16 * G
F32 = jnp.float32
BF16 = jnp.bfloat16


def split_bf16(value):
    high = value.astype(BF16)
    return high, (value - high.astype(F32)).astype(BF16)


def pick_taps(taps_ref, count, offset):
    out = jnp.zeros(offset.shape, F32)
    for k in range(count):
        out = jnp.where(offset == k, taps_ref[k], out)
    return out


def wrap(offset):
    return jnp.where(offset < 0, offset + G, jnp.where(offset >= G, offset - G, offset))


def ints(shape, dim):
    return lax.broadcasted_iota(jnp.int32, shape, dim)


def div_g(value):
    return (value * 1366) >> 16


def x_matrix(taps_ref, count, rows, transposed):
    shape = (rows, rows)
    r, c = ints(shape, 0), ints(shape, 1)
    gap = (r >> 2) - (c >> 2) if transposed else (c >> 2) - (r >> 2)
    offset = wrap(gap + (count - 1) // 2)
    return jnp.where((r & 3) == (c & 3), pick_taps(taps_ref, count, offset), 0.0)


def z_table(taps_ref, count, transposed):
    shape = (G, BLK)
    lane = ints(shape, 1)
    z_out = lane - G * div_g(lane)
    z_in = ints(shape, 0)
    gap = z_out - z_in if transposed else z_in - z_out
    return pick_taps(taps_ref, count, wrap(gap + (count - 1) // 2))


def y_table(taps_ref, count, reach, transposed):
    shape = (16 + 2 * reach, BLK)
    gap = ints(shape, 0) - reach - div_g(ints(shape, 1))
    if transposed:
        gap = -gap
    return pick_taps(taps_ref, count, gap + (count - 1) // 2)


def h_kernel(magic_ref, kinetic_ref, psi_ref, pot_ref, out_ref,
             s, t, zt, zt2, yt, w_hi, w_lo, lhs, prod, pad, xm):
    rows = s.shape[0]
    n_magic, n_kin = magic_ref.shape[0], kinetic_ref.shape[0]

    def fill_weights(depth, with_identity):
        def body(j, carry):
            value = zt[...] * yt[pl.ds(j, 1), :]
            if with_identity:
                lane = ints((1, BLK), 1)
                same = jnp.where(div_g(lane) == j - 16, 1.0, 0.0).astype(F32)
                value = value + zt2[...] * same
            high, low = split_bf16(value)
            at = pl.multiple_of(j * G, G)
            w_hi[pl.ds(at, G), :] = high
            w_lo[pl.ds(at, G), :] = low
            return carry
        lax.fori_loop(0, depth, body, 0)

    def fill_lhs(source, reach):
        edge = reach * G
        width = (16 + 2 * reach) * G
        for part in range(2):
            pad[:, 0:PLANE] = split_bf16(source[...])[part]
            pad[:, PLANE:2 * PLANE] = pad[:, 0:PLANE]
            for n in range(3):
                start = (BLK * n - edge) % PLANE
                lhs[pl.ds((3 * part + n) * rows, rows), 0:width] = pad[:, start:start + width]

    def kron(width, accumulate, target):
        def body(nt, carry):
            at = pl.multiple_of(nt * 256, 256)
            cols = pl.ds(at, 256)
            prod[...] = jnp.dot(lhs[:, 0:width], w_hi[0:width, cols], preferred_element_type=F32)
            low = jnp.dot(lhs[0:3 * rows, 0:width], w_lo[0:width, cols], preferred_element_type=F32)
            for n in range(3):
                value = (prod[n * rows:(n + 1) * rows, :] + prod[(3 + n) * rows:(4 + n) * rows, :]
                         + low[n * rows:(n + 1) * rows, :])
                place = pl.ds(pl.multiple_of(BLK * n + nt * 256, 256), 256)
                if accumulate:
                    value = value + target[:, place]
                target[:, place] = value
            return carry
        lax.fori_loop(0, 3, body, 0)

    def along_x(matrix, source, finish):
        high, low = split_bf16(matrix)
        xm[0:rows, :] = high
        xm[rows:, :] = low

        def body(nt, carry):
            cols = pl.ds(pl.multiple_of(nt * 256, 256), 256)
            b_hi, b_lo = split_bf16(source[:, cols])
            both = jnp.dot(xm[...], b_hi, preferred_element_type=F32)
            low = jnp.dot(xm[0:rows, :], b_lo, preferred_element_type=F32)
            finish(cols, both[0:rows] + both[rows:] + low)
            return carry
        lax.fori_loop(0, PLANE // 256, body, 0)

    for x in range(G):
        s[4 * x:4 * x + 4, :] = psi_ref[:, x * PLANE:(x + 1) * PLANE]

    zt[...] = z_table(magic_ref, n_magic, False)
    yt[0:32, :] = y_table(magic_ref, n_magic, 8, False)
    fill_weights(32, False)
    fill_lhs(s, 8)
    kron(2 * BLK, False, t)

    def magic_and_potential(cols, value):
        pot = pot_ref[:, cols]
        t[:, cols] = value * jnp.broadcast_to(pot[:, None, :], (G, 4, 256)).reshape(rows, 256)

    along_x(x_matrix(magic_ref, n_magic, rows, False), t, magic_and_potential)

    def keep(cols, value):
        t[:, cols] = value

    along_x(x_matrix(magic_ref, n_magic, rows, True), t, keep)

    zt[...] = z_table(magic_ref, n_magic, True)
    yt[0:32, :] = y_table(magic_ref, n_magic, 8, True)
    fill_weights(32, False)
    fill_lhs(t, 8)

    def start_sum(cols, value):
        t[:, cols] = value

    along_x(x_matrix(kinetic_ref, n_kin, rows, False), s, start_sum)
    kron(2 * BLK, True, t)

    shape = (G, BLK)
    lane = ints(shape, 1)
    zt[...] = jnp.where(lane - G * div_g(lane) == ints(shape, 0), 1.0, 0.0).astype(F32)
    zt2[...] = z_table(kinetic_ref, n_kin, False)
    yt[...] = y_table(kinetic_ref, n_kin, 16, False)
    fill_weights(48, True)
    fill_lhs(s, 16)
    kron(3 * BLK, True, t)

    for x in range(G):
        out_ref[:, x * PLANE:(x + 1) * PLANE] = t[4 * x:4 * x + 4, :]


def hamiltonian(orbitals, potential, magic_taps, kinetic_taps):
    count = orbitals.shape[0]
    rows = count * G
    vmem = pl.BlockSpec(memory_space=pltpu.VMEM)
    smem = pl.BlockSpec(memory_space=pltpu.SMEM)
    return pl.pallas_call(
        h_kernel,
        out_shape=jax.ShapeDtypeStruct(orbitals.shape, F32),
        in_specs=[smem, smem, vmem, vmem],
        out_specs=vmem,
        scratch_shapes=[
            pltpu.VMEM((rows, PLANE), F32),
            pltpu.VMEM((rows, PLANE), F32),
            pltpu.VMEM((G, BLK), F32),
            pltpu.VMEM((G, BLK), F32),
            pltpu.VMEM((G, BLK), F32),
            pltpu.VMEM((PLANE, BLK), BF16),
            pltpu.VMEM((PLANE, BLK), BF16),
            pltpu.VMEM((6 * rows, PLANE), BF16),
            pltpu.VMEM((6 * rows, 256), F32),
            pltpu.VMEM((rows, 2 * PLANE), BF16),
            pltpu.VMEM((2 * rows, rows), BF16),
        ],
        compiler_params=pltpu.CompilerParams(vmem_limit_bytes=48 * 1024 * 1024),
        cost_estimate=pl.CostEstimate(
            flops=24_000_000_000, transcendentals=0, bytes_accessed=12 * orbitals.size
        ),
        name="hamiltonian",
    )(magic_taps, kinetic_taps, orbitals, potential.reshape(G, PLANE))


def to_cols(block):
    pieces = block.reshape(block.shape[0], NSPLIT, -1).transpose(1, 0, 2)
    return lax.all_to_all(pieces, COEF, split_axis=0, concat_axis=0, tiled=True)


def flat(pieces):
    return pieces.reshape(-1, pieces.shape[-1])


def step_x(pieces, step):
    return lax.ppermute(pieces, "x", [(i, (i + step) % 4) for i in range(4)])


def swap_core(value):
    return lax.ppermute(value, "core", [(0, 1), (1, 0)])


def shards(orbitals, potential, magic_taps, kinetic_taps):
    own = to_cols(orbitals)
    hpsi = hamiltonian(orbitals, potential, magic_taps, kinetic_taps)
    own, hpsi = lax.optimization_barrier((own, hpsi))
    left, right = step_x(own, 1), step_x(own, -1)
    hpsi_cols = to_cols(hpsi)
    half = NSPLIT // 2
    far_a, far_b = step_x(left[:half], 1), step_x(right[half:], -1)
    hpsi_swap = swap_core(hpsi_cols)
    both = jnp.concatenate([flat(hpsi_cols), flat(hpsi_swap)], axis=0)
    panels = [flat(v) for v in (own, left, right, far_a, far_b)]
    part = jnp.concatenate(
        [jnp.einsum("jc,ic->ji", psi, both, precision=HIGH) for psi in panels], axis=0
    ) * (1.0 / NC)
    rows = part.shape[0] // NSPLIT
    terms = lax.all_to_all(
        part.reshape(NSPLIT, rows, -1), COEF, split_axis=0, concat_axis=0, tiled=True
    )
    mine = jnp.sum(terms, axis=0)
    margin = lax.all_to_all(
        jnp.broadcast_to(mine[None], terms.shape), COEF, split_axis=0, concat_axis=0, tiled=True
    ).reshape(part.shape)
    stack = jnp.concatenate(panels, axis=0)
    cols = margin.shape[1] // 2
    other = jnp.einsum("ji,jc->ic", margin[:, cols:], stack, precision=HIGH)
    from_other = swap_core(other)
    grad_cols = flat(hpsi_cols) - jnp.einsum("ji,jc->ic", margin[:, :cols], stack, precision=HIGH) - from_other
    back = lax.all_to_all(
        grad_cols.reshape(hpsi_cols.shape), COEF, split_axis=0, concat_axis=0, tiled=True
    )
    return back.transpose(1, 0, 2).reshape(orbitals.shape)


def solution(mesh):
    fine = Mesh(mesh.devices.reshape(SPLIT), NAMES)
    placed = (P(NAMES, None), P(), P(), P())
    return jax.shard_map(
        shards, mesh=fine, in_specs=placed, out_specs=P(NAMES, None), check_vma=False
    )
```

```python
import functools

import jax
import jax.numpy as jnp
from jax import lax
from jax.experimental import pallas as pl
from jax.experimental.pallas import tpu as pltpu
from jax.sharding import Mesh, PartitionSpec as P

G = 48
NC = 110592
SPLIT = (4, 2, 4, 2, 4)
NAMES = ("x", "zl", "y", "core", "zh")
COEF = ("y", "zl", "zh")
NSPLIT = 32
CHUNK = 384
PLANE = G * G
BLK = 16 * G
F32 = jnp.float32
BF16 = jnp.bfloat16


def split_bf16(value):
    high = value.astype(BF16)
    return high, (value - high.astype(F32)).astype(BF16)


def pick_taps(taps_ref, count, offset):
    out = jnp.zeros(offset.shape, F32)
    for k in range(count):
        out = jnp.where(offset == k, taps_ref[k], out)
    return out


def wrap(offset):
    return jnp.where(offset < 0, offset + G, jnp.where(offset >= G, offset - G, offset))


def ints(shape, dim):
    return lax.broadcasted_iota(jnp.int32, shape, dim)


def div_g(value):
    return (value * 1366) >> 16


def x_matrix(taps_ref, count, rows, transposed):
    shape = (rows, rows)
    r, c = ints(shape, 0), ints(shape, 1)
    gap = (r >> 2) - (c >> 2) if transposed else (c >> 2) - (r >> 2)
    offset = wrap(gap + (count - 1) // 2)
    return jnp.where((r & 3) == (c & 3), pick_taps(taps_ref, count, offset), 0.0)


def z_table(taps_ref, count, transposed):
    shape = (G, BLK)
    lane = ints(shape, 1)
    z_out = lane - G * div_g(lane)
    z_in = ints(shape, 0)
    gap = z_out - z_in if transposed else z_in - z_out
    return pick_taps(taps_ref, count, wrap(gap + (count - 1) // 2))


def y_table(taps_ref, count, reach, transposed):
    shape = (16 + 2 * reach, BLK)
    gap = ints(shape, 0) - reach - div_g(ints(shape, 1))
    if transposed:
        gap = -gap
    return pick_taps(taps_ref, count, gap + (count - 1) // 2)


def h_kernel(magic_ref, kinetic_ref, psi_ref, pot_ref, out_ref,
             s, t, zt, zt2, yt, w_hi, w_lo, lhs, prod, pad, xm):
    rows = s.shape[0]
    n_magic, n_kin = magic_ref.shape[0], kinetic_ref.shape[0]

    def fill_weights(depth, with_identity):
        def body(j, carry):
            value = zt[...] * yt[pl.ds(j, 1), :]
            if with_identity:
                lane = ints((1, BLK), 1)
                same = jnp.where(div_g(lane) == j - 16, 1.0, 0.0).astype(F32)
                value = value + zt2[...] * same
            high, low = split_bf16(value)
            at = pl.multiple_of(j * G, G)
            w_hi[pl.ds(at, G), :] = high
            w_lo[pl.ds(at, G), :] = low
            return carry
        lax.fori_loop(0, depth, body, 0)

    def fill_lhs(source, reach):
        edge = reach * G
        width = (16 + 2 * reach) * G
        for part in range(2):
            pad[:, 0:PLANE] = split_bf16(source[...])[part]
            pad[:, PLANE:2 * PLANE] = pad[:, 0:PLANE]
            for n in range(3):
                start = (BLK * n - edge) % PLANE
                lhs[pl.ds((3 * part + n) * rows, rows), 0:width] = pad[:, start:start + width]

    def kron(width, accumulate, target):
        def body(nt, carry):
            at = pl.multiple_of(nt * 256, 256)
            cols = pl.ds(at, 256)
            prod[...] = jnp.dot(lhs[:, 0:width], w_hi[0:width, cols], preferred_element_type=F32)
            low = jnp.dot(lhs[0:3 * rows, 0:width], w_lo[0:width, cols], preferred_element_type=F32)
            for n in range(3):
                value = (prod[n * rows:(n + 1) * rows, :] + prod[(3 + n) * rows:(4 + n) * rows, :]
                         + low[n * rows:(n + 1) * rows, :])
                place = pl.ds(pl.multiple_of(BLK * n + nt * 256, 256), 256)
                if accumulate:
                    value = value + target[:, place]
                target[:, place] = value
            return carry
        lax.fori_loop(0, 3, body, 0)

    def along_x(matrix, source, finish):
        high, low = split_bf16(matrix)
        xm[0:rows, :] = high
        xm[rows:, :] = low

        def body(nt, carry):
            cols = pl.ds(pl.multiple_of(nt * 256, 256), 256)
            b_hi, b_lo = split_bf16(source[:, cols])
            both = jnp.dot(xm[...], b_hi, preferred_element_type=F32)
            low = jnp.dot(xm[0:rows, :], b_lo, preferred_element_type=F32)
            finish(cols, both[0:rows] + both[rows:] + low)
            return carry
        lax.fori_loop(0, PLANE // 256, body, 0)

    for x in range(G):
        s[4 * x:4 * x + 4, :] = psi_ref[:, x * PLANE:(x + 1) * PLANE]

    zt[...] = z_table(magic_ref, n_magic, False)
    yt[0:32, :] = y_table(magic_ref, n_magic, 8, False)
    fill_weights(32, False)
    fill_lhs(s, 8)
    kron(2 * BLK, False, t)

    def magic_and_potential(cols, value):
        pot = pot_ref[:, cols]
        t[:, cols] = value * jnp.broadcast_to(pot[:, None, :], (G, 4, 256)).reshape(rows, 256)

    along_x(x_matrix(magic_ref, n_magic, rows, False), t, magic_and_potential)

    def keep(cols, value):
        t[:, cols] = value

    along_x(x_matrix(magic_ref, n_magic, rows, True), t, keep)

    zt[...] = z_table(magic_ref, n_magic, True)
    yt[0:32, :] = y_table(magic_ref, n_magic, 8, True)
    fill_weights(32, False)
    fill_lhs(t, 8)

    def start_sum(cols, value):
        t[:, cols] = value

    along_x(x_matrix(kinetic_ref, n_kin, rows, False), s, start_sum)
    kron(2 * BLK, True, t)

    shape = (G, BLK)
    lane = ints(shape, 1)
    zt[...] = jnp.where(lane - G * div_g(lane) == ints(shape, 0), 1.0, 0.0).astype(F32)
    zt2[...] = z_table(kinetic_ref, n_kin, False)
    yt[...] = y_table(kinetic_ref, n_kin, 16, False)
    fill_weights(48, True)
    fill_lhs(s, 16)
    kron(3 * BLK, True, t)

    for x in range(G):
        out_ref[:, x * PLANE:(x + 1) * PLANE] = t[4 * x:4 * x + 4, :]


def hamiltonian(orbitals, potential, magic_taps, kinetic_taps):
    count = orbitals.shape[0]
    rows = count * G
    vmem = pl.BlockSpec(memory_space=pltpu.VMEM)
    smem = pl.BlockSpec(memory_space=pltpu.SMEM)
    return pl.pallas_call(
        h_kernel,
        out_shape=jax.ShapeDtypeStruct(orbitals.shape, F32),
        in_specs=[smem, smem, vmem, vmem],
        out_specs=vmem,
        scratch_shapes=[
            pltpu.VMEM((rows, PLANE), F32),
            pltpu.VMEM((rows, PLANE), F32),
            pltpu.VMEM((G, BLK), F32),
            pltpu.VMEM((G, BLK), F32),
            pltpu.VMEM((G, BLK), F32),
            pltpu.VMEM((PLANE, BLK), BF16),
            pltpu.VMEM((PLANE, BLK), BF16),
            pltpu.VMEM((6 * rows, PLANE), BF16),
            pltpu.VMEM((6 * rows, 256), F32),
            pltpu.VMEM((rows, 2 * PLANE), BF16),
            pltpu.VMEM((2 * rows, rows), BF16),
        ],
        compiler_params=pltpu.CompilerParams(vmem_limit_bytes=48 * 1024 * 1024),
        cost_estimate=pl.CostEstimate(
            flops=24_000_000_000, transcendentals=0, bytes_accessed=12 * orbitals.size
        ),
        name="hamiltonian",
    )(magic_taps, kinetic_taps, orbitals, potential.reshape(G, PLANE))


def to_cols(block):
    pieces = block.reshape(block.shape[0], NSPLIT, -1).transpose(1, 0, 2)
    return lax.all_to_all(pieces, COEF, split_axis=0, concat_axis=0, tiled=True)


def step_x(pieces, step):
    return lax.ppermute(pieces, "x", [(i, (i + step) % 4) for i in range(4)])


def swap_core(value):
    return lax.ppermute(value, "core", [(0, 1), (1, 0)])


def rows_of(ref, scratch, start):
    count = ref.shape[0]
    for s in range(count):
        scratch[start + 4 * s:start + 4 * s + 4, :] = ref[s]


NT = (((1,), (1,)), ((), ()))


def margin_kernel(*refs):
    panels, (own_ref, swap_ref, out_ref, psi, hps) = refs[:-5], refs[-5:]
    rows_of(own_ref, hps, 0)
    rows_of(swap_ref, hps, hps.shape[0] // 2)
    at = 0
    for ref in panels:
        rows_of(ref, psi, at)
        at += 4 * ref.shape[0]
    h_hi, h_lo = split_bf16(hps[...])
    p_hi, p_lo = split_bf16(psi[...])

    def times(a, b):
        return lax.dot_general(a, b, NT, preferred_element_type=F32)

    total = (times(p_hi, h_hi) + times(p_hi, h_lo) + times(p_lo, h_hi)) * (1.0 / NC)

    @pl.when(pl.program_id(0) == 0)
    def _():
        out_ref[...] = total

    @pl.when(pl.program_id(0) > 0)
    def _():
        out_ref[...] += total


def chunk_spec(array):
    return pl.BlockSpec((array.shape[0], array.shape[1], CHUNK), lambda k: (0, 0, k))


def margin_part(panels, own, swap):
    rows = sum(4 * v.shape[0] for v in panels)
    cols = 8 * own.shape[0]
    width = own.shape[2]
    arrays = [*panels, own, swap]
    return pl.pallas_call(
        margin_kernel,
        grid=(width // CHUNK,),
        out_shape=jax.ShapeDtypeStruct((rows, cols), F32),
        in_specs=[chunk_spec(v) for v in arrays],
        out_specs=pl.BlockSpec((rows, cols), lambda k: (0, 0)),
        scratch_shapes=[pltpu.VMEM((rows, CHUNK), F32), pltpu.VMEM((cols, CHUNK), F32)],
        cost_estimate=pl.CostEstimate(
            flops=6 * rows * cols * width, transcendentals=0, bytes_accessed=4 * (rows + cols) * width
        ),
        compiler_params=pltpu.CompilerParams(vmem_limit_bytes=40 * 1024 * 1024),
        name="margin_part",
    )(*arrays)


def rotate_kernel(column, negate, *refs):
    if negate:
        base_ref, out_ref, psi, turn, res = refs[-5:]
        panels = refs[1:-5]
    else:
        out_ref, psi, turn, res = refs[-4:]
        panels = refs[1:-4]
    margin_ref = refs[0]
    cols = turn.shape[0] // 2

    @pl.when(pl.program_id(0) == 0)
    def _():
        high, low = split_bf16(margin_ref[:, column * cols:(column + 1) * cols].T)
        turn[0:cols, :] = high
        turn[cols:, :] = low

    at = 0
    for ref in panels:
        rows_of(ref, psi, at)
        at += 4 * ref.shape[0]
    p_hi, p_lo = split_bf16(psi[...])
    both = jnp.dot(turn[...], p_hi, preferred_element_type=F32)
    res[...] = both[0:cols] + both[cols:] + jnp.dot(turn[0:cols, :], p_lo, preferred_element_type=F32)
    for s in range(out_ref.shape[0]):
        value = res[4 * s:4 * s + 4, :]
        out_ref[s] = base_ref[s] - value if negate else value


def rotated(margin, panels, column, base=None):
    rows, cols = margin.shape[0], margin.shape[1] // 2
    shape = (cols // 4, 4, panels[0].shape[2])
    arrays = [*panels] + ([] if base is None else [base])
    return pl.pallas_call(
        functools.partial(rotate_kernel, column, base is not None),
        grid=(shape[2] // CHUNK,),
        out_shape=jax.ShapeDtypeStruct(shape, F32),
        in_specs=[pl.BlockSpec(margin.shape, lambda k: (0, 0))] + [chunk_spec(v) for v in arrays],
        out_specs=pl.BlockSpec((shape[0], 4, CHUNK), lambda k: (0, 0, k)),
        scratch_shapes=[
            pltpu.VMEM((rows, CHUNK), F32),
            pltpu.VMEM((2 * cols, rows), BF16),
            pltpu.VMEM((cols, CHUNK), F32),
        ],
        cost_estimate=pl.CostEstimate(
            flops=6 * rows * cols * shape[2], transcendentals=0,
            bytes_accessed=4 * (rows + 2 * cols) * shape[2],
        ),
        compiler_params=pltpu.CompilerParams(vmem_limit_bytes=40 * 1024 * 1024),
        name="rotated",
    )(margin, *arrays)


def shards(orbitals, potential, magic_taps, kinetic_taps):
    own = to_cols(orbitals)
    hpsi = hamiltonian(orbitals, potential, magic_taps, kinetic_taps)
    own, hpsi = lax.optimization_barrier((own, hpsi))
    left, right = step_x(own, 1), step_x(own, -1)
    hpsi_cols = to_cols(hpsi)
    half = NSPLIT // 2
    far_a, far_b = step_x(left[:half], 1), step_x(right[half:], -1)
    hpsi_swap = swap_core(hpsi_cols)
    near = margin_part([own, left, right], hpsi_cols, hpsi_swap)
    far = margin_part([far_a, far_b], hpsi_cols, hpsi_swap)
    part = jnp.concatenate([near, far], axis=0)
    rows = part.shape[0] // NSPLIT
    terms = lax.all_to_all(
        part.reshape(NSPLIT, rows, -1), COEF, split_axis=0, concat_axis=0, tiled=True
    )
    mine = jnp.sum(terms, axis=0)
    margin = lax.all_to_all(
        jnp.broadcast_to(mine[None], terms.shape), COEF, split_axis=0, concat_axis=0, tiled=True
    ).reshape(part.shape)
    panels = [own, left, right, far_a, far_b]
    from_other = swap_core(rotated(margin, panels, 1))
    grad_cols = rotated(margin, panels, 0, hpsi_cols) - from_other
    back = lax.all_to_all(grad_cols, COEF, split_axis=0, concat_axis=0, tiled=True)
    return back.transpose(1, 0, 2).reshape(orbitals.shape)


def solution(mesh):
    fine = Mesh(mesh.devices.reshape(SPLIT), NAMES)
    placed = (P(NAMES, None), P(), P(), P())
    return jax.shard_map(
        shards, mesh=fine, in_specs=placed, out_specs=P(NAMES, None), check_vma=False
    )
```

```python
import jax
import jax.numpy as jnp
from jax import lax
from jax.experimental import pallas as pl
from jax.experimental.pallas import tpu as pltpu
from jax.sharding import Mesh, PartitionSpec as P

G = 48
NC = 110592
SPLIT = (4, 2, 4, 2, 4)
NAMES = ("x", "zl", "y", "core", "zh")
COEF = ("y", "zl", "zh")
NSPLIT = 32
CHUNK = 1152
WIDE = 1152
PLANE = G * G
BLK = 16 * G
F32 = jnp.float32
BF16 = jnp.bfloat16


def split_bf16(value):
    high = value.astype(BF16)
    return high, (value - high.astype(F32)).astype(BF16)


def pick_taps(taps_ref, count, offset):
    out = jnp.zeros(offset.shape, F32)
    for k in range(count):
        out = jnp.where(offset == k, taps_ref[k], out)
    return out


def wrap(offset):
    return jnp.where(offset < 0, offset + G, jnp.where(offset >= G, offset - G, offset))


def ints(shape, dim):
    return lax.broadcasted_iota(jnp.int32, shape, dim)


def div_g(value):
    return (value * 1366) >> 16


def x_matrix(taps_ref, count, rows, transposed):
    shape = (rows, rows)
    r, c = ints(shape, 0), ints(shape, 1)
    gap = (r >> 2) - (c >> 2) if transposed else (c >> 2) - (r >> 2)
    offset = wrap(gap + (count - 1) // 2)
    return jnp.where((r & 3) == (c & 3), pick_taps(taps_ref, count, offset), 0.0)


def z_table(taps_ref, count, transposed):
    shape = (G, BLK)
    lane = ints(shape, 1)
    z_out = lane - G * div_g(lane)
    z_in = ints(shape, 0)
    gap = z_out - z_in if transposed else z_in - z_out
    return pick_taps(taps_ref, count, wrap(gap + (count - 1) // 2))


def y_table(taps_ref, count, reach, transposed):
    shape = (16 + 2 * reach, BLK)
    gap = ints(shape, 0) - reach - div_g(ints(shape, 1))
    if transposed:
        gap = -gap
    return pick_taps(taps_ref, count, gap + (count - 1) // 2)


def h_kernel(magic_ref, kinetic_ref, psi_ref, pot_ref, out_ref,
             s, t, zt, zt2, yt, w_hi, w_lo, lhs, prod, pad, xm):
    rows = s.shape[0]
    n_magic, n_kin = magic_ref.shape[0], kinetic_ref.shape[0]

    def fill_weights(depth, with_identity):
        def body(j, carry):
            value = zt[...] * yt[pl.ds(j, 1), :]
            if with_identity:
                lane = ints((1, BLK), 1)
                same = jnp.where(div_g(lane) == j - 16, 1.0, 0.0).astype(F32)
                value = value + zt2[...] * same
            high, low = split_bf16(value)
            at = pl.multiple_of(j * G, G)
            w_hi[pl.ds(at, G), :] = high
            w_lo[pl.ds(at, G), :] = low
            return carry
        lax.fori_loop(0, depth, body, 0)

    def fill_lhs(source, reach):
        edge = reach * G
        width = (16 + 2 * reach) * G
        for part in range(2):
            pad[:, 0:PLANE] = split_bf16(source[...])[part]
            pad[:, PLANE:2 * PLANE] = pad[:, 0:PLANE]
            for n in range(3):
                start = (BLK * n - edge) % PLANE
                lhs[pl.ds((3 * part + n) * rows, rows), 0:width] = pad[:, start:start + width]

    def kron(width, accumulate, target):
        def body(nt, carry):
            at = pl.multiple_of(nt * 256, 256)
            cols = pl.ds(at, 256)
            prod[...] = jnp.dot(lhs[:, 0:width], w_hi[0:width, cols], preferred_element_type=F32)
            low = jnp.dot(lhs[0:3 * rows, 0:width], w_lo[0:width, cols], preferred_element_type=F32)
            for n in range(3):
                value = (prod[n * rows:(n + 1) * rows, :] + prod[(3 + n) * rows:(4 + n) * rows, :]
                         + low[n * rows:(n + 1) * rows, :])
                place = pl.ds(pl.multiple_of(BLK * n + nt * 256, 256), 256)
                if accumulate:
                    value = value + target[:, place]
                target[:, place] = value
            return carry
        lax.fori_loop(0, 3, body, 0)

    def along_x(matrix, source, finish):
        high, low = split_bf16(matrix)
        xm[0:rows, :] = high
        xm[rows:, :] = low

        def body(nt, carry):
            cols = pl.ds(pl.multiple_of(nt * 256, 256), 256)
            b_hi, b_lo = split_bf16(source[:, cols])
            both = jnp.dot(xm[...], b_hi, preferred_element_type=F32)
            low = jnp.dot(xm[0:rows, :], b_lo, preferred_element_type=F32)
            finish(cols, both[0:rows] + both[rows:] + low)
            return carry
        lax.fori_loop(0, PLANE // 256, body, 0)

    for x in range(G):
        s[4 * x:4 * x + 4, :] = psi_ref[:, x * PLANE:(x + 1) * PLANE]

    zt[...] = z_table(magic_ref, n_magic, False)
    yt[0:32, :] = y_table(magic_ref, n_magic, 8, False)
    fill_weights(32, False)
    fill_lhs(s, 8)
    kron(2 * BLK, False, t)

    def magic_and_potential(cols, value):
        pot = pot_ref[:, cols]
        t[:, cols] = value * jnp.broadcast_to(pot[:, None, :], (G, 4, 256)).reshape(rows, 256)

    along_x(x_matrix(magic_ref, n_magic, rows, False), t, magic_and_potential)

    def keep(cols, value):
        t[:, cols] = value

    along_x(x_matrix(magic_ref, n_magic, rows, True), t, keep)

    zt[...] = z_table(magic_ref, n_magic, True)
    yt[0:32, :] = y_table(magic_ref, n_magic, 8, True)
    fill_weights(32, False)
    fill_lhs(t, 8)

    def start_sum(cols, value):
        t[:, cols] = value

    along_x(x_matrix(kinetic_ref, n_kin, rows, False), s, start_sum)
    kron(2 * BLK, True, t)

    shape = (G, BLK)
    lane = ints(shape, 1)
    zt[...] = jnp.where(lane - G * div_g(lane) == ints(shape, 0), 1.0, 0.0).astype(F32)
    zt2[...] = z_table(kinetic_ref, n_kin, False)
    yt[...] = y_table(kinetic_ref, n_kin, 16, False)
    fill_weights(48, True)
    fill_lhs(s, 16)
    kron(3 * BLK, True, t)

    for x in range(G):
        out_ref[:, x * PLANE:(x + 1) * PLANE] = t[4 * x:4 * x + 4, :]


def hamiltonian(orbitals, potential, magic_taps, kinetic_taps):
    count = orbitals.shape[0]
    rows = count * G
    vmem = pl.BlockSpec(memory_space=pltpu.VMEM)
    smem = pl.BlockSpec(memory_space=pltpu.SMEM)
    return pl.pallas_call(
        h_kernel,
        out_shape=jax.ShapeDtypeStruct(orbitals.shape, F32),
        in_specs=[smem, smem, vmem, vmem],
        out_specs=vmem,
        scratch_shapes=[
            pltpu.VMEM((rows, PLANE), F32),
            pltpu.VMEM((rows, PLANE), F32),
            pltpu.VMEM((G, BLK), F32),
            pltpu.VMEM((G, BLK), F32),
            pltpu.VMEM((G, BLK), F32),
            pltpu.VMEM((PLANE, BLK), BF16),
            pltpu.VMEM((PLANE, BLK), BF16),
            pltpu.VMEM((6 * rows, PLANE), BF16),
            pltpu.VMEM((6 * rows, 256), F32),
            pltpu.VMEM((rows, 2 * PLANE), BF16),
            pltpu.VMEM((2 * rows, rows), BF16),
        ],
        compiler_params=pltpu.CompilerParams(vmem_limit_bytes=36 * 1024 * 1024),
        cost_estimate=pl.CostEstimate(
            flops=24_000_000_000, transcendentals=0, bytes_accessed=12 * orbitals.size
        ),
        name="hamiltonian",
    )(magic_taps, kinetic_taps, orbitals, potential.reshape(G, PLANE))


def exchange(pieces):
    return lax.all_to_all(pieces, COEF, split_axis=0, concat_axis=0, tiled=True)


def to_cols(block):
    pieces = block.reshape(block.shape[0], NSPLIT, -1).transpose(1, 0, 2)
    return exchange(pieces)


def sum_over_cols(part):
    return jnp.sum(exchange(part.reshape(NSPLIT, -1, part.shape[1])), axis=0)


def step_x(pieces, step):
    return lax.ppermute(pieces, "x", [(i, (i + step) % 4) for i in range(4)])


def swap_core(value):
    return lax.ppermute(value, "core", [(0, 1), (1, 0)])


def rows_of(ref, scratch, start):
    count = ref.shape[0]
    for s in range(count):
        scratch[start + 4 * s:start + 4 * s + 4, :] = ref[s]


NT = (((1,), (1,)), ((), ()))


def margin_kernel(*refs):
    panels, (own_ref, swap_ref, out_ref, high_ref, low_ref, psi, hps, hsp) = refs[:-8], refs[-8:]
    rows_of(own_ref, hps, 0)
    rows_of(swap_ref, hps, hps.shape[0] // 2)
    at = 0
    for ref in panels:
        rows_of(ref, psi, at)
        at += 4 * ref.shape[0]
    cols = hps.shape[0]
    high, low = split_bf16(hps[...])
    hsp[0:cols, :] = high
    hsp[cols:, :] = low
    p_hi, p_lo = split_bf16(psi[...])
    high_ref[...] = p_hi
    low_ref[...] = p_lo
    both = lax.dot_general(hsp[...], p_hi, NT, preferred_element_type=F32)
    cross = lax.dot_general(hsp[0:cols, :], p_lo, NT, preferred_element_type=F32)
    total = (both[0:cols] + both[cols:] + cross) * (1.0 / NC)

    @pl.when(pl.program_id(0) == 0)
    def _():
        out_ref[...] = total

    @pl.when(pl.program_id(0) > 0)
    def _():
        out_ref[...] += total


def chunk_spec(array, chunk):
    return pl.BlockSpec((*array.shape[:-1], chunk), lambda k: (0,) * (len(array.shape) - 1) + (k,))


def margin_part(panels, own, swap):
    rows = sum(4 * v.shape[0] for v in panels)
    cols = 8 * own.shape[0]
    width = own.shape[2]
    arrays = [*panels, own, swap]
    half = jax.ShapeDtypeStruct((rows, width), BF16)
    return pl.pallas_call(
        margin_kernel,
        grid=(width // CHUNK,),
        out_shape=[jax.ShapeDtypeStruct((cols, rows), F32), half, half],
        in_specs=[chunk_spec(v, CHUNK) for v in arrays],
        out_specs=[pl.BlockSpec((cols, rows), lambda k: (0, 0))] + [chunk_spec(half, CHUNK)] * 2,
        scratch_shapes=[
            pltpu.VMEM((rows, CHUNK), F32),
            pltpu.VMEM((cols, CHUNK), F32),
            pltpu.VMEM((2 * cols, CHUNK), BF16),
        ],
        cost_estimate=pl.CostEstimate(
            flops=6 * rows * cols * width, transcendentals=0,
            bytes_accessed=4 * (2 * rows + cols) * width,
        ),
        compiler_params=pltpu.CompilerParams(vmem_limit_bytes=24 * 1024 * 1024),
        name="margin_part",
    )(*arrays)


def rotate_kernel(margin_ref, *refs):
    halves, (base_ref, mine_ref, other_ref, turn, res) = refs[:-5], refs[-5:]
    cols = margin_ref.shape[0]

    @pl.when(pl.program_id(0) == 0)
    def _():
        high, low = split_bf16(margin_ref[...])
        turn[0:cols, :] = high
        turn[cols:, :] = low

    at = 0
    total = None
    for high_ref, low_ref in zip(halves[::2], halves[1::2]):
        upto = at + high_ref.shape[0]
        both = jnp.dot(turn[:, at:upto], high_ref[...], preferred_element_type=F32)
        low = jnp.dot(turn[0:cols, at:upto], low_ref[...], preferred_element_type=F32)
        value = both[0:cols] + both[cols:] + low
        total = value if total is None else total + value
        at = upto
    res[...] = total
    for s in range(mine_ref.shape[0]):
        mine_ref[s] = base_ref[s] - res[4 * s:4 * s + 4, :]
        other_ref[s] = res[cols // 2 + 4 * s:cols // 2 + 4 * s + 4, :]


def rotated(margin, halves, base):
    cols, rows = margin.shape
    width = base.shape[2]
    shape = jax.ShapeDtypeStruct(base.shape, F32)
    return pl.pallas_call(
        rotate_kernel,
        grid=(width // WIDE,),
        out_shape=[shape, shape],
        in_specs=[pl.BlockSpec(margin.shape, lambda k: (0, 0))]
        + [chunk_spec(v, WIDE) for v in (*halves, base)],
        out_specs=[chunk_spec(base, WIDE)] * 2,
        scratch_shapes=[pltpu.VMEM((2 * cols, rows), BF16), pltpu.VMEM((cols, WIDE), F32)],
        cost_estimate=pl.CostEstimate(
            flops=6 * rows * cols * width, transcendentals=0,
            bytes_accessed=4 * (rows + 2 * cols) * width,
        ),
        compiler_params=pltpu.CompilerParams(vmem_limit_bytes=24 * 1024 * 1024),
        name="rotated",
    )(margin, *halves, base)


def shards(orbitals, potential, magic_taps, kinetic_taps):
    own = to_cols(orbitals)
    hpsi = hamiltonian(orbitals, potential, magic_taps, kinetic_taps)
    own, _ = lax.optimization_barrier((own, hpsi))
    left, right = step_x(own, 1), step_x(own, -1)
    hpsi_cols = to_cols(hpsi)
    half = NSPLIT // 2
    far_a, far_b = step_x(left[:half], 1), step_x(right[half:], -1)
    hpsi_swap = swap_core(hpsi_cols)
    near, *near_halves = margin_part([own, left, right], hpsi_cols, hpsi_swap)
    far, *far_halves = margin_part([far_a, far_b], hpsi_cols, hpsi_swap)
    mine = jnp.concatenate([sum_over_cols(near), sum_over_cols(far)], axis=1)
    margin = exchange(jnp.broadcast_to(mine[None], (NSPLIT, *mine.shape))).reshape(-1, mine.shape[1])
    grad_mine, grad_other = rotated(margin, near_halves + far_halves, hpsi_cols)
    grad_cols = grad_mine - swap_core(grad_other)
    back = exchange(grad_cols)
    return back.transpose(1, 0, 2).reshape(orbitals.shape)


def solution(mesh):
    fine = Mesh(mesh.devices.reshape(SPLIT), NAMES)
    placed = (P(NAMES, None), P(), P(), P())
    return jax.shard_map(
        shards, mesh=fine, in_specs=placed, out_specs=P(NAMES, None), check_vma=False
    )
```

```python
import jax
import jax.numpy as jnp
from jax import lax
from jax.experimental import pallas as pl
from jax.experimental.pallas import tpu as pltpu
from jax.sharding import Mesh, PartitionSpec as P

G = 48
NC = 110592
SPLIT = (4, 2, 4, 2, 4)
NAMES = ("x", "zl", "y", "core", "zh")
COEF = ("y", "zl", "zh")
NSPLIT = 32
CHUNK = 1152
WIDE = 1152
PLANE = G * G
BLK = 16 * G
F32 = jnp.float32
BF16 = jnp.bfloat16


def split_bf16(value):
    high = value.astype(BF16)
    return high, (value - high.astype(F32)).astype(BF16)


def pick_taps(taps_ref, count, offset):
    out = jnp.zeros(offset.shape, F32)
    for k in range(count):
        out = jnp.where(offset == k, taps_ref[k], out)
    return out


def wrap(offset):
    return jnp.where(offset < 0, offset + G, jnp.where(offset >= G, offset - G, offset))


def ints(shape, dim):
    return lax.broadcasted_iota(jnp.int32, shape, dim)


def div_g(value):
    return (value * 1366) >> 16


def x_matrix(taps_ref, count, rows, transposed):
    shape = (rows, rows)
    r, c = ints(shape, 0), ints(shape, 1)
    gap = (r >> 2) - (c >> 2) if transposed else (c >> 2) - (r >> 2)
    offset = wrap(gap + (count - 1) // 2)
    return jnp.where((r & 3) == (c & 3), pick_taps(taps_ref, count, offset), 0.0)


def z_table(taps_ref, count, transposed):
    shape = (G, BLK)
    lane = ints(shape, 1)
    z_out = lane - G * div_g(lane)
    z_in = ints(shape, 0)
    gap = z_out - z_in if transposed else z_in - z_out
    return pick_taps(taps_ref, count, wrap(gap + (count - 1) // 2))


def y_table(taps_ref, count, reach, transposed):
    shape = (16 + 2 * reach, BLK)
    gap = ints(shape, 0) - reach - div_g(ints(shape, 1))
    if transposed:
        gap = -gap
    return pick_taps(taps_ref, count, gap + (count - 1) // 2)


def h_kernel(magic_ref, kinetic_ref, psi_ref, pot_ref, out_ref,
             s, t, zt, zt2, yt, w_hi, w_lo, lhs, prod, pad, xm):
    rows = s.shape[0]
    n_magic, n_kin = magic_ref.shape[0], kinetic_ref.shape[0]

    def fill_weights(depth, with_identity):
        def body(j, carry):
            value = zt[...] * yt[pl.ds(j, 1), :]
            if with_identity:
                lane = ints((1, BLK), 1)
                same = jnp.where(div_g(lane) == j - 16, 1.0, 0.0).astype(F32)
                value = value + zt2[...] * same
            high, low = split_bf16(value)
            at = pl.multiple_of(j * G, G)
            w_hi[pl.ds(at, G), :] = high
            w_lo[pl.ds(at, G), :] = low
            return carry
        lax.fori_loop(0, depth, body, 0)

    def fill_lhs(source, reach):
        edge = reach * G
        width = (16 + 2 * reach) * G
        for part in range(2):
            pad[:, 0:PLANE] = split_bf16(source[...])[part]
            pad[:, PLANE:2 * PLANE] = pad[:, 0:PLANE]
            for n in range(3):
                start = (BLK * n - edge) % PLANE
                lhs[pl.ds((3 * part + n) * rows, rows), 0:width] = pad[:, start:start + width]

    def kron(width, accumulate, target):
        def body(nt, carry):
            at = pl.multiple_of(nt * 256, 256)
            cols = pl.ds(at, 256)
            prod[...] = jnp.dot(lhs[:, 0:width], w_hi[0:width, cols], preferred_element_type=F32)
            low = jnp.dot(lhs[0:3 * rows, 0:width], w_lo[0:width, cols], preferred_element_type=F32)
            for n in range(3):
                value = (prod[n * rows:(n + 1) * rows, :] + prod[(3 + n) * rows:(4 + n) * rows, :]
                         + low[n * rows:(n + 1) * rows, :])
                place = pl.ds(pl.multiple_of(BLK * n + nt * 256, 256), 256)
                if accumulate:
                    value = value + target[:, place]
                target[:, place] = value
            return carry
        lax.fori_loop(0, 3, body, 0)

    def along_x(matrix, source, finish):
        high, low = split_bf16(matrix)
        xm[0:rows, :] = high
        xm[rows:, :] = low

        def body(nt, carry):
            cols = pl.ds(pl.multiple_of(nt * 256, 256), 256)
            b_hi, b_lo = split_bf16(source[:, cols])
            both = jnp.dot(xm[...], b_hi, preferred_element_type=F32)
            low = jnp.dot(xm[0:rows, :], b_lo, preferred_element_type=F32)
            finish(cols, both[0:rows] + both[rows:] + low)
            return carry
        lax.fori_loop(0, PLANE // 256, body, 0)

    for x in range(G):
        s[4 * x:4 * x + 4, :] = psi_ref[:, x * PLANE:(x + 1) * PLANE]

    zt[...] = z_table(magic_ref, n_magic, False)
    yt[0:32, :] = y_table(magic_ref, n_magic, 8, False)
    fill_weights(32, False)
    fill_lhs(s, 8)
    kron(2 * BLK, False, t)

    def magic_and_potential(cols, value):
        pot = pot_ref[:, cols]
        t[:, cols] = value * jnp.broadcast_to(pot[:, None, :], (G, 4, 256)).reshape(rows, 256)

    along_x(x_matrix(magic_ref, n_magic, rows, False), t, magic_and_potential)

    def keep(cols, value):
        t[:, cols] = value

    along_x(x_matrix(magic_ref, n_magic, rows, True), t, keep)

    zt[...] = z_table(magic_ref, n_magic, True)
    yt[0:32, :] = y_table(magic_ref, n_magic, 8, True)
    fill_weights(32, False)
    fill_lhs(t, 8)

    def start_sum(cols, value):
        t[:, cols] = value

    along_x(x_matrix(kinetic_ref, n_kin, rows, False), s, start_sum)
    kron(2 * BLK, True, t)

    shape = (G, BLK)
    lane = ints(shape, 1)
    zt[...] = jnp.where(lane - G * div_g(lane) == ints(shape, 0), 1.0, 0.0).astype(F32)
    zt2[...] = z_table(kinetic_ref, n_kin, False)
    yt[...] = y_table(kinetic_ref, n_kin, 16, False)
    fill_weights(48, True)
    fill_lhs(s, 16)
    kron(3 * BLK, True, t)

    for x in range(G):
        out_ref[:, x * PLANE:(x + 1) * PLANE] = t[4 * x:4 * x + 4, :]


def hamiltonian(orbitals, potential, magic_taps, kinetic_taps):
    count = orbitals.shape[0]
    rows = count * G
    vmem = pl.BlockSpec(memory_space=pltpu.VMEM)
    smem = pl.BlockSpec(memory_space=pltpu.SMEM)
    return pl.pallas_call(
        h_kernel,
        out_shape=jax.ShapeDtypeStruct(orbitals.shape, F32),
        in_specs=[smem, smem, vmem, vmem],
        out_specs=vmem,
        scratch_shapes=[
            pltpu.VMEM((rows, PLANE), F32),
            pltpu.VMEM((rows, PLANE), F32),
            pltpu.VMEM((G, BLK), F32),
            pltpu.VMEM((G, BLK), F32),
            pltpu.VMEM((G, BLK), F32),
            pltpu.VMEM((PLANE, BLK), BF16),
            pltpu.VMEM((PLANE, BLK), BF16),
            pltpu.VMEM((6 * rows, PLANE), BF16),
            pltpu.VMEM((6 * rows, 256), F32),
            pltpu.VMEM((rows, 2 * PLANE), BF16),
            pltpu.VMEM((2 * rows, rows), BF16),
        ],
        compiler_params=pltpu.CompilerParams(vmem_limit_bytes=36 * 1024 * 1024),
        cost_estimate=pl.CostEstimate(
            flops=24_000_000_000, transcendentals=0, bytes_accessed=12 * orbitals.size
        ),
        name="hamiltonian",
    )(magic_taps, kinetic_taps, orbitals, potential.reshape(G, PLANE))


def exchange(pieces):
    return lax.all_to_all(pieces, COEF, split_axis=0, concat_axis=0, tiled=True)


def to_cols(block):
    pieces = block.reshape(block.shape[0], NSPLIT, -1).transpose(1, 0, 2)
    return exchange(pieces)


def step_x(pieces, step):
    return lax.ppermute(pieces, "x", [(i, (i + step) % 4) for i in range(4)])


def swap_core(value):
    return lax.ppermute(value, "core", [(0, 1), (1, 0)])


def rows_of(ref, scratch, start):
    count = ref.shape[0]
    for s in range(count):
        scratch[start + 4 * s:start + 4 * s + 4, :] = ref[s]


NT = (((1,), (1,)), ((), ()))


def add_up(out, place, total):
    @pl.when(pl.program_id(0) == 0)
    def _():
        out[:, place] = total

    @pl.when(pl.program_id(0) > 0)
    def _():
        out[:, place] += total


def margin_terms(panels, psi, hsp_ref, high_ref, low_ref):
    at = 0
    for ref in panels:
        rows_of(ref, psi, at)
        at += 4 * ref.shape[0]
    cols = hsp_ref.shape[0] // 2
    p_hi, p_lo = split_bf16(psi[...])
    high_ref[...] = p_hi
    low_ref[...] = p_lo
    both = lax.dot_general(hsp_ref[...], p_hi, NT, preferred_element_type=F32)
    cross = lax.dot_general(hsp_ref[0:cols, :], p_lo, NT, preferred_element_type=F32)
    return (both[0:cols] + both[cols:] + cross) * (1.0 / NC)


def near_kernel(*refs):
    panels, (own_ref, swap_ref, out_ref, high_ref, low_ref, hsp_ref, psi, hps) = refs[:-8], refs[-8:]
    cols = hps.shape[0]
    rows_of(own_ref, hps, 0)
    rows_of(swap_ref, hps, cols // 2)
    high, low = split_bf16(hps[...])
    hsp_ref[0:cols, :] = high
    hsp_ref[cols:, :] = low
    add_up(out_ref, slice(None), margin_terms(panels, psi, hsp_ref, high_ref, low_ref))


def far_kernel(near_ref, hsp_ref, *refs):
    panels, (out_ref, high_ref, low_ref, psi) = refs[:-4], refs[-4:]
    start = near_ref.shape[1]

    @pl.when(pl.program_id(0) == 0)
    def _():
        out_ref[:, 0:start] = near_ref[...]

    add_up(out_ref, slice(start, None), margin_terms(panels, psi, hsp_ref, high_ref, low_ref))


def chunk_spec(array, chunk):
    return pl.BlockSpec((*array.shape[:-1], chunk), lambda k: (0,) * (len(array.shape) - 1) + (k,))


def in_hbm(rows, width):
    return pltpu.MemorySpace.HBM((rows, width), BF16)


def margin_call(kernel, rows, cols, out_cols, extra, whole, arrays, outs, name):
    width = arrays[-1].shape[-1]
    return pl.pallas_call(
        kernel,
        grid=(width // CHUNK,),
        out_shape=[jax.ShapeDtypeStruct((cols, out_cols), F32)] + [in_hbm(r, width) for r in outs],
        in_specs=[pl.BlockSpec(v.shape, lambda k: (0, 0)) for v in whole]
        + [chunk_spec(v, CHUNK) for v in arrays],
        out_specs=[pl.BlockSpec((cols, out_cols), lambda k: (0, 0))]
        + [pl.BlockSpec((r, CHUNK), lambda k: (0, k)) for r in outs],
        scratch_shapes=[pltpu.VMEM((rows, CHUNK), F32)] + extra,
        cost_estimate=pl.CostEstimate(
            flops=6 * rows * cols * width, transcendentals=0,
            bytes_accessed=4 * (2 * rows + 2 * cols) * width,
        ),
        compiler_params=pltpu.CompilerParams(vmem_limit_bytes=32 * 1024 * 1024),
        name=name,
    )(*whole, *arrays)


def rows_in(panels):
    return sum(4 * v.shape[0] for v in panels)


def near_part(panels, own, swap):
    rows, cols = rows_in(panels), rows_in([own, swap])
    return margin_call(
        near_kernel, rows, cols, rows, [pltpu.VMEM((cols, CHUNK), F32)], [],
        [*panels, own, swap], [rows, rows, 2 * cols], "near_part",
    )


def far_part(near, hsp, panels):
    rows, cols = rows_in(panels), near.shape[0]
    return margin_call(
        far_kernel, rows, cols, near.shape[1] + rows, [], [near], [hsp, *panels], [rows, rows], "far_part",
    )


def rotate_kernel(margin_ref, *refs):
    halves, (base_ref, mine_ref, other_ref, turn, res) = refs[:-5], refs[-5:]
    cols = margin_ref.shape[0]

    @pl.when(pl.program_id(0) == 0)
    def _():
        high, low = split_bf16(margin_ref[...])
        turn[0:cols, :] = high
        turn[cols:, :] = low

    at = 0
    total = None
    for high_ref, low_ref in zip(halves[::2], halves[1::2]):
        upto = at + high_ref.shape[0]
        both = jnp.dot(turn[:, at:upto], high_ref[...], preferred_element_type=F32)
        low = jnp.dot(turn[0:cols, at:upto], low_ref[...], preferred_element_type=F32)
        value = both[0:cols] + both[cols:] + low
        total = value if total is None else total + value
        at = upto
    res[...] = total
    for s in range(mine_ref.shape[0]):
        mine_ref[s] = base_ref[s] - res[4 * s:4 * s + 4, :]
        other_ref[s] = res[cols // 2 + 4 * s:cols // 2 + 4 * s + 4, :]


def rotated(margin, halves, base):
    cols, rows = margin.shape
    width = base.shape[2]
    shape = jax.ShapeDtypeStruct(base.shape, F32)
    return pl.pallas_call(
        rotate_kernel,
        grid=(width // WIDE,),
        out_shape=[shape, shape],
        in_specs=[pl.BlockSpec(margin.shape, lambda k: (0, 0))]
        + [chunk_spec(v, WIDE) for v in (*halves, base)],
        out_specs=[chunk_spec(base, WIDE)] * 2,
        scratch_shapes=[pltpu.VMEM((2 * cols, rows), BF16), pltpu.VMEM((cols, WIDE), F32)],
        cost_estimate=pl.CostEstimate(
            flops=6 * rows * cols * width, transcendentals=0,
            bytes_accessed=4 * (rows + 2 * cols) * width,
        ),
        compiler_params=pltpu.CompilerParams(vmem_limit_bytes=24 * 1024 * 1024),
        name="rotated",
    )(margin, *halves, base)


def shards(orbitals, potential, magic_taps, kinetic_taps):
    own = to_cols(orbitals)
    hpsi = hamiltonian(orbitals, potential, magic_taps, kinetic_taps)
    own, _ = lax.optimization_barrier((own, hpsi))
    left, right = step_x(own, 1), step_x(own, -1)
    hpsi_cols = to_cols(hpsi)
    half = NSPLIT // 2
    far_a, far_b = step_x(left[:half], 1), step_x(right[half:], -1)
    hpsi_swap = swap_core(hpsi_cols)
    near, *near_halves, hsp = near_part([own, left, right], hpsi_cols, hpsi_swap)
    part, *far_halves = far_part(near, hsp, [far_a, far_b])
    mine = jnp.sum(exchange(part.reshape(NSPLIT, -1, part.shape[1])), axis=0)
    margin = exchange(jnp.broadcast_to(mine[None], (NSPLIT, *mine.shape))).reshape(part.shape)
    grad_mine, grad_other = rotated(margin, near_halves + far_halves, hpsi_cols)
    grad_cols = grad_mine - swap_core(grad_other)
    back = exchange(grad_cols)
    return back.transpose(1, 0, 2).reshape(orbitals.shape)


def solution(mesh):
    fine = Mesh(mesh.devices.reshape(SPLIT), NAMES)
    placed = (P(NAMES, None), P(), P(), P())
    return jax.shard_map(
        shards, mesh=fine, in_specs=placed, out_specs=P(NAMES, None), check_vma=False
    )
```

```python
import jax
import jax.numpy as jnp
from jax import lax
from jax.experimental import pallas as pl
from jax.experimental.pallas import tpu as pltpu
from jax.sharding import Mesh, PartitionSpec as P

G = 48
NC = 110592
SPLIT = (4, 2, 4, 2, 4)
NAMES = ("x", "zl", "y", "core", "zh")
COEF = ("y", "zl", "zh")
NSPLIT = 32
CHUNK = 1152
WIDE = 1152
VMEM_MOST = 58 * 1024 * 1024
PLANE = G * G
BLK = 16 * G
F32 = jnp.float32
BF16 = jnp.bfloat16


def split_bf16(value):
    high = value.astype(BF16)
    return high, (value - high.astype(F32)).astype(BF16)


def pick_taps(taps_ref, count, offset):
    out = jnp.zeros(offset.shape, F32)
    for k in range(count):
        out = jnp.where(offset == k, taps_ref[k], out)
    return out


def wrap(offset):
    return jnp.where(offset < 0, offset + G, jnp.where(offset >= G, offset - G, offset))


def ints(shape, dim):
    return lax.broadcasted_iota(jnp.int32, shape, dim)


def div_g(value):
    return (value * 1366) >> 16


def x_matrix(taps_ref, count, rows, transposed):
    shape = (rows, rows)
    r, c = ints(shape, 0), ints(shape, 1)
    gap = (r >> 2) - (c >> 2) if transposed else (c >> 2) - (r >> 2)
    offset = wrap(gap + (count - 1) // 2)
    return jnp.where((r & 3) == (c & 3), pick_taps(taps_ref, count, offset), 0.0)


def z_table(taps_ref, count, transposed):
    shape = (G, BLK)
    lane = ints(shape, 1)
    z_out = lane - G * div_g(lane)
    z_in = ints(shape, 0)
    gap = z_out - z_in if transposed else z_in - z_out
    return pick_taps(taps_ref, count, wrap(gap + (count - 1) // 2))


def y_table(taps_ref, count, reach, transposed):
    shape = (16 + 2 * reach, BLK)
    gap = ints(shape, 0) - reach - div_g(ints(shape, 1))
    if transposed:
        gap = -gap
    return pick_taps(taps_ref, count, gap + (count - 1) // 2)


def h_kernel(magic_ref, kinetic_ref, psi_ref, pot_ref, out_ref,
             s, t, zt, zt2, yt, w_hi, w_lo, lhs, prod, pad, xm):
    rows = s.shape[0]
    n_magic, n_kin = magic_ref.shape[0], kinetic_ref.shape[0]

    def fill_weights(depth, with_identity):
        def body(j, carry):
            value = zt[...] * yt[pl.ds(j, 1), :]
            if with_identity:
                lane = ints((1, BLK), 1)
                same = jnp.where(div_g(lane) == j - 16, 1.0, 0.0).astype(F32)
                value = value + zt2[...] * same
            high, low = split_bf16(value)
            at = pl.multiple_of(j * G, G)
            w_hi[pl.ds(at, G), :] = high
            w_lo[pl.ds(at, G), :] = low
            return carry
        lax.fori_loop(0, depth, body, 0)

    def fill_lhs(source, reach):
        edge = reach * G
        width = (16 + 2 * reach) * G
        for part in range(2):
            pad[:, 0:PLANE] = split_bf16(source[...])[part]
            pad[:, PLANE:2 * PLANE] = pad[:, 0:PLANE]
            for n in range(3):
                start = (BLK * n - edge) % PLANE
                lhs[pl.ds((3 * part + n) * rows, rows), 0:width] = pad[:, start:start + width]

    def kron(width, accumulate, target):
        def body(nt, carry):
            at = pl.multiple_of(nt * 256, 256)
            cols = pl.ds(at, 256)
            prod[...] = jnp.dot(lhs[:, 0:width], w_hi[0:width, cols], preferred_element_type=F32)
            low = jnp.dot(lhs[0:3 * rows, 0:width], w_lo[0:width, cols], preferred_element_type=F32)
            for n in range(3):
                value = (prod[n * rows:(n + 1) * rows, :] + prod[(3 + n) * rows:(4 + n) * rows, :]
                         + low[n * rows:(n + 1) * rows, :])
                place = pl.ds(pl.multiple_of(BLK * n + nt * 256, 256), 256)
                if accumulate:
                    value = value + target[:, place]
                target[:, place] = value
            return carry
        lax.fori_loop(0, 3, body, 0)

    def along_x(matrix, source, finish):
        high, low = split_bf16(matrix)
        xm[0:rows, :] = high
        xm[rows:, :] = low

        def body(nt, carry):
            cols = pl.ds(pl.multiple_of(nt * 256, 256), 256)
            b_hi, b_lo = split_bf16(source[:, cols])
            both = jnp.dot(xm[...], b_hi, preferred_element_type=F32)
            low = jnp.dot(xm[0:rows, :], b_lo, preferred_element_type=F32)
            finish(cols, both[0:rows] + both[rows:] + low)
            return carry
        lax.fori_loop(0, PLANE // 256, body, 0)

    for x in range(G):
        s[4 * x:4 * x + 4, :] = psi_ref[:, x * PLANE:(x + 1) * PLANE]

    zt[...] = z_table(magic_ref, n_magic, False)
    yt[0:32, :] = y_table(magic_ref, n_magic, 8, False)
    fill_weights(32, False)
    fill_lhs(s, 8)
    kron(2 * BLK, False, t)

    def magic_and_potential(cols, value):
        pot = pot_ref[:, cols]
        t[:, cols] = value * jnp.broadcast_to(pot[:, None, :], (G, 4, 256)).reshape(rows, 256)

    along_x(x_matrix(magic_ref, n_magic, rows, False), t, magic_and_potential)

    def keep(cols, value):
        t[:, cols] = value

    along_x(x_matrix(magic_ref, n_magic, rows, True), t, keep)

    zt[...] = z_table(magic_ref, n_magic, True)
    yt[0:32, :] = y_table(magic_ref, n_magic, 8, True)
    fill_weights(32, False)
    fill_lhs(t, 8)

    def start_sum(cols, value):
        t[:, cols] = value

    along_x(x_matrix(kinetic_ref, n_kin, rows, False), s, start_sum)
    kron(2 * BLK, True, t)

    shape = (G, BLK)
    lane = ints(shape, 1)
    zt[...] = jnp.where(lane - G * div_g(lane) == ints(shape, 0), 1.0, 0.0).astype(F32)
    zt2[...] = z_table(kinetic_ref, n_kin, False)
    yt[...] = y_table(kinetic_ref, n_kin, 16, False)
    fill_weights(48, True)
    fill_lhs(s, 16)
    kron(3 * BLK, True, t)

    for x in range(G):
        out_ref[:, x * PLANE:(x + 1) * PLANE] = t[4 * x:4 * x + 4, :]


def hamiltonian(orbitals, potential, magic_taps, kinetic_taps):
    count = orbitals.shape[0]
    rows = count * G
    vmem = pl.BlockSpec(memory_space=pltpu.VMEM)
    smem = pl.BlockSpec(memory_space=pltpu.SMEM)
    return pl.pallas_call(
        h_kernel,
        out_shape=jax.ShapeDtypeStruct(orbitals.shape, F32),
        in_specs=[smem, smem, vmem, vmem],
        out_specs=vmem,
        scratch_shapes=[
            pltpu.VMEM((rows, PLANE), F32),
            pltpu.VMEM((rows, PLANE), F32),
            pltpu.VMEM((G, BLK), F32),
            pltpu.VMEM((G, BLK), F32),
            pltpu.VMEM((G, BLK), F32),
            pltpu.VMEM((PLANE, BLK), BF16),
            pltpu.VMEM((PLANE, BLK), BF16),
            pltpu.VMEM((6 * rows, PLANE), BF16),
            pltpu.VMEM((6 * rows, 256), F32),
            pltpu.VMEM((rows, 2 * PLANE), BF16),
            pltpu.VMEM((2 * rows, rows), BF16),
        ],
        compiler_params=pltpu.CompilerParams(vmem_limit_bytes=36 * 1024 * 1024),
        cost_estimate=pl.CostEstimate(
            flops=24_000_000_000, transcendentals=0, bytes_accessed=12 * orbitals.size
        ),
        name="hamiltonian",
    )(magic_taps, kinetic_taps, orbitals, potential.reshape(G, PLANE))


def exchange(pieces):
    return lax.all_to_all(pieces, COEF, split_axis=0, concat_axis=0, tiled=True)


def to_cols(block):
    pieces = block.reshape(block.shape[0], NSPLIT, -1).transpose(1, 0, 2)
    return exchange(pieces)


def step_x(pieces, step):
    return lax.ppermute(pieces, "x", [(i, (i + step) % 4) for i in range(4)])


def swap_core(value):
    return lax.ppermute(value, "core", [(0, 1), (1, 0)])


def rows_of(ref, scratch, start):
    count = ref.shape[0]
    for s in range(count):
        scratch[start + 4 * s:start + 4 * s + 4, :] = ref[s]


NT = (((1,), (1,)), ((), ()))


def add_up(out, place, total):
    @pl.when(pl.program_id(0) == 0)
    def _():
        out[:, place] = total

    @pl.when(pl.program_id(0) > 0)
    def _():
        out[:, place] += total


def margin_terms(panels, psi, hsp_ref, high_ref, low_ref):
    at = 0
    for ref in panels:
        rows_of(ref, psi, at)
        at += 4 * ref.shape[0]
    cols = hsp_ref.shape[0] // 2
    p_hi, p_lo = split_bf16(psi[...])
    high_ref[...] = p_hi
    low_ref[...] = p_lo
    both = lax.dot_general(hsp_ref[...], p_hi, NT, preferred_element_type=F32)
    cross = lax.dot_general(hsp_ref[0:cols, :], p_lo, NT, preferred_element_type=F32)
    return (both[0:cols] + both[cols:] + cross) * (1.0 / NC)


def near_kernel(*refs):
    panels, (own_ref, swap_ref, out_ref, high_ref, low_ref, hsp_ref, psi, hps) = refs[:-8], refs[-8:]
    cols = hps.shape[0]
    rows_of(own_ref, hps, 0)
    rows_of(swap_ref, hps, cols // 2)
    high, low = split_bf16(hps[...])
    hsp_ref[0:cols, :] = high
    hsp_ref[cols:, :] = low
    add_up(out_ref, slice(None), margin_terms(panels, psi, hsp_ref, high_ref, low_ref))


def far_kernel(near_ref, hsp_ref, *refs):
    panels, (out_ref, high_ref, low_ref, psi) = refs[:-4], refs[-4:]
    start = near_ref.shape[1]

    @pl.when(pl.program_id(0) == 0)
    def _():
        out_ref[:, 0:start] = near_ref[...]

    add_up(out_ref, slice(start, None), margin_terms(panels, psi, hsp_ref, high_ref, low_ref))


def chunk_spec(array, chunk):
    return pl.BlockSpec((*array.shape[:-1], chunk), lambda k: (0,) * (len(array.shape) - 1) + (k,))


def in_hbm(rows, width):
    return pltpu.MemorySpace.HBM((rows, width), BF16)


def margin_call(kernel, rows, cols, out_cols, extra, whole, arrays, outs, name):
    width = arrays[-1].shape[-1]
    return pl.pallas_call(
        kernel,
        grid=(width // CHUNK,),
        out_shape=[jax.ShapeDtypeStruct((cols, out_cols), F32)] + outs(width),
        in_specs=[pl.BlockSpec(v.shape, lambda k: (0, 0)) for v in whole]
        + [chunk_spec(v, CHUNK) for v in arrays],
        out_specs=[pl.BlockSpec((cols, out_cols), lambda k: (0, 0))]
        + [chunk_spec(v, CHUNK) for v in outs(width)],
        scratch_shapes=[pltpu.VMEM((rows, CHUNK), F32)] + extra,
        cost_estimate=pl.CostEstimate(
            flops=6 * rows * cols * width, transcendentals=0,
            bytes_accessed=4 * (2 * rows + 2 * cols) * width,
        ),
        compiler_params=pltpu.CompilerParams(vmem_limit_bytes=24 * 1024 * 1024),
        name=name,
    )(*whole, *arrays)


def rows_in(panels):
    return sum(4 * v.shape[0] for v in panels)


def near_part(panels, own, swap):
    rows, cols = rows_in(panels), rows_in([own, swap])
    return margin_call(
        near_kernel, rows, cols, rows, [pltpu.VMEM((cols, CHUNK), F32)], [],
        [*panels, own, swap], lambda w: [in_hbm(rows, w)] * 2 + [jax.ShapeDtypeStruct((2 * cols, w), BF16)], "near_part",
    )


def far_part(near, hsp, panels):
    rows, cols = rows_in(panels), near.shape[0]
    return margin_call(
        far_kernel, rows, cols, near.shape[1] + rows, [], [near], [hsp, *panels],
        lambda w: [in_hbm(rows, w)] * 2, "far_part",
    )


def rotate_kernel(margin_ref, *refs):
    halves, (base_ref, mine_ref, other_ref, turn, res) = refs[:-5], refs[-5:]
    cols = margin_ref.shape[0]

    @pl.when(pl.program_id(0) == 0)
    def _():
        high, low = split_bf16(margin_ref[...])
        turn[0:cols, :] = high
        turn[cols:, :] = low

    at = 0
    total = None
    for high_ref, low_ref in zip(halves[::2], halves[1::2]):
        upto = at + high_ref.shape[0]
        both = jnp.dot(turn[:, at:upto], high_ref[...], preferred_element_type=F32)
        low = jnp.dot(turn[0:cols, at:upto], low_ref[...], preferred_element_type=F32)
        value = both[0:cols] + both[cols:] + low
        total = value if total is None else total + value
        at = upto
    res[...] = total
    for s in range(mine_ref.shape[0]):
        mine_ref[s] = base_ref[s] - res[4 * s:4 * s + 4, :]
        other_ref[s] = res[cols // 2 + 4 * s:cols // 2 + 4 * s + 4, :]


def rotated(margin, halves, base):
    cols, rows = margin.shape
    width = base.shape[2]
    shape = jax.ShapeDtypeStruct(base.shape, F32)
    return pl.pallas_call(
        rotate_kernel,
        grid=(width // WIDE,),
        out_shape=[shape, shape],
        in_specs=[pl.BlockSpec(margin.shape, lambda k: (0, 0))]
        + [chunk_spec(v, WIDE) for v in (*halves, base)],
        out_specs=[chunk_spec(base, WIDE)] * 2,
        scratch_shapes=[pltpu.VMEM((2 * cols, rows), BF16), pltpu.VMEM((cols, WIDE), F32)],
        cost_estimate=pl.CostEstimate(
            flops=6 * rows * cols * width, transcendentals=0,
            bytes_accessed=4 * (rows + 2 * cols) * width,
        ),
        compiler_params=pltpu.CompilerParams(vmem_limit_bytes=VMEM_MOST),
        name="rotated",
    )(margin, *halves, base)


def shards(orbitals, potential, magic_taps, kinetic_taps):
    own = to_cols(orbitals)
    hpsi = hamiltonian(orbitals, potential, magic_taps, kinetic_taps)
    own, _ = lax.optimization_barrier((own, hpsi))
    left, right = step_x(own, 1), step_x(own, -1)
    hpsi_cols = to_cols(hpsi)
    half = NSPLIT // 2
    from_left, from_right = left[:half], right[half:]
    far_a, far_b = step_x(from_left, 1), step_x(from_right, -1)
    hpsi_cols, _, _ = lax.optimization_barrier((hpsi_cols, from_left, from_right))
    hpsi_swap = swap_core(hpsi_cols)
    near, *near_halves, hsp = near_part([own, left, right], hpsi_cols, hpsi_swap)
    part, *far_halves = far_part(near, hsp, [far_a, far_b])
    mine = jnp.sum(exchange(part.reshape(NSPLIT, -1, part.shape[1])), axis=0)
    margin = exchange(jnp.broadcast_to(mine[None], (NSPLIT, *mine.shape))).reshape(part.shape)
    grad_mine, grad_other = rotated(margin, near_halves + far_halves, hpsi_cols)
    grad_cols = grad_mine - swap_core(grad_other)
    back = exchange(grad_cols)
    return back.transpose(1, 0, 2).reshape(orbitals.shape)


def solution(mesh):
    fine = Mesh(mesh.devices.reshape(SPLIT), NAMES)
    placed = (P(NAMES, None), P(), P(), P())
    return jax.shard_map(
        shards, mesh=fine, in_specs=placed, out_specs=P(NAMES, None), check_vma=False
    )
```

```python
import jax
import jax.numpy as jnp
from jax import lax
from jax.experimental import pallas as pl
from jax.experimental.pallas import tpu as pltpu
from jax.sharding import Mesh, PartitionSpec as P

G = 48
NC = 110592
SPLIT = (4, 2, 4, 2, 4)
NAMES = ("x", "zl", "y", "core", "zh")
COEF = ("y", "zl", "zh")
NSPLIT = 32
CHUNK = 1152
WIDE = 1152
PLANE = G * G
BLK = 16 * G
F32 = jnp.float32
BF16 = jnp.bfloat16


def split_bf16(value):
    high = value.astype(BF16)
    return high, (value - high.astype(F32)).astype(BF16)


def pick_taps(taps_ref, count, offset):
    out = jnp.zeros(offset.shape, F32)
    for k in range(count):
        out = jnp.where(offset == k, taps_ref[k], out)
    return out


def wrap(offset):
    return jnp.where(offset < 0, offset + G, jnp.where(offset >= G, offset - G, offset))


def ints(shape, dim):
    return lax.broadcasted_iota(jnp.int32, shape, dim)


def div_g(value):
    return (value * 1366) >> 16


def x_matrix(taps_ref, count, rows, transposed):
    shape = (rows, rows)
    r, c = ints(shape, 0), ints(shape, 1)
    gap = (r >> 2) - (c >> 2) if transposed else (c >> 2) - (r >> 2)
    offset = wrap(gap + (count - 1) // 2)
    return jnp.where((r & 3) == (c & 3), pick_taps(taps_ref, count, offset), 0.0)


def z_table(taps_ref, count, transposed):
    shape = (G, BLK)
    lane = ints(shape, 1)
    z_out = lane - G * div_g(lane)
    z_in = ints(shape, 0)
    gap = z_out - z_in if transposed else z_in - z_out
    return pick_taps(taps_ref, count, wrap(gap + (count - 1) // 2))


def y_table(taps_ref, count, reach, transposed):
    shape = (16 + 2 * reach, BLK)
    gap = ints(shape, 0) - reach - div_g(ints(shape, 1))
    if transposed:
        gap = -gap
    return pick_taps(taps_ref, count, gap + (count - 1) // 2)


def h_kernel(magic_ref, kinetic_ref, psi_ref, pot_ref, out_ref,
             s, t, zt, zt2, yt, w_hi, w_lo, lhs, prod, pad, xm):
    rows = s.shape[0]
    n_magic, n_kin = magic_ref.shape[0], kinetic_ref.shape[0]

    def fill_weights(depth, with_identity):
        def body(j, carry):
            value = zt[...] * yt[pl.ds(j, 1), :]
            if with_identity:
                lane = ints((1, BLK), 1)
                same = jnp.where(div_g(lane) == j - 16, 1.0, 0.0).astype(F32)
                value = value + zt2[...] * same
            high, low = split_bf16(value)
            at = pl.multiple_of(j * G, G)
            w_hi[pl.ds(at, G), :] = high
            w_lo[pl.ds(at, G), :] = low
            return carry
        lax.fori_loop(0, depth, body, 0)

    def fill_lhs(source, reach):
        edge = reach * G
        width = (16 + 2 * reach) * G
        for part in range(2):
            pad[:, 0:PLANE] = split_bf16(source[...])[part]
            pad[:, PLANE:2 * PLANE] = pad[:, 0:PLANE]
            for n in range(3):
                start = (BLK * n - edge) % PLANE
                lhs[pl.ds((3 * part + n) * rows, rows), 0:width] = pad[:, start:start + width]

    def kron(width, accumulate, target):
        def body(nt, carry):
            at = pl.multiple_of(nt * 256, 256)
            cols = pl.ds(at, 256)
            prod[...] = jnp.dot(lhs[:, 0:width], w_hi[0:width, cols], preferred_element_type=F32)
            low = jnp.dot(lhs[0:3 * rows, 0:width], w_lo[0:width, cols], preferred_element_type=F32)
            for n in range(3):
                value = (prod[n * rows:(n + 1) * rows, :] + prod[(3 + n) * rows:(4 + n) * rows, :]
                         + low[n * rows:(n + 1) * rows, :])
                place = pl.ds(pl.multiple_of(BLK * n + nt * 256, 256), 256)
                if accumulate:
                    value = value + target[:, place]
                target[:, place] = value
            return carry
        lax.fori_loop(0, 3, body, 0)

    def along_x(matrix, source, finish):
        high, low = split_bf16(matrix)
        xm[0:rows, :] = high
        xm[rows:, :] = low

        def body(nt, carry):
            cols = pl.ds(pl.multiple_of(nt * 256, 256), 256)
            b_hi, b_lo = split_bf16(source[:, cols])
            both = jnp.dot(xm[...], b_hi, preferred_element_type=F32)
            low = jnp.dot(xm[0:rows, :], b_lo, preferred_element_type=F32)
            finish(cols, both[0:rows] + both[rows:] + low)
            return carry
        lax.fori_loop(0, PLANE // 256, body, 0)

    for x in range(G):
        s[4 * x:4 * x + 4, :] = psi_ref[:, x * PLANE:(x + 1) * PLANE]

    zt[...] = z_table(magic_ref, n_magic, False)
    yt[0:32, :] = y_table(magic_ref, n_magic, 8, False)
    fill_weights(32, False)
    fill_lhs(s, 8)
    kron(2 * BLK, False, t)

    def magic_and_potential(cols, value):
        pot = pot_ref[:, cols]
        t[:, cols] = value * jnp.broadcast_to(pot[:, None, :], (G, 4, 256)).reshape(rows, 256)

    along_x(x_matrix(magic_ref, n_magic, rows, False), t, magic_and_potential)

    def keep(cols, value):
        t[:, cols] = value

    along_x(x_matrix(magic_ref, n_magic, rows, True), t, keep)

    zt[...] = z_table(magic_ref, n_magic, True)
    yt[0:32, :] = y_table(magic_ref, n_magic, 8, True)
    fill_weights(32, False)
    fill_lhs(t, 8)

    def start_sum(cols, value):
        t[:, cols] = value

    along_x(x_matrix(kinetic_ref, n_kin, rows, False), s, start_sum)
    kron(2 * BLK, True, t)

    shape = (G, BLK)
    lane = ints(shape, 1)
    zt[...] = jnp.where(lane - G * div_g(lane) == ints(shape, 0), 1.0, 0.0).astype(F32)
    zt2[...] = z_table(kinetic_ref, n_kin, False)
    yt[...] = y_table(kinetic_ref, n_kin, 16, False)
    fill_weights(48, True)
    fill_lhs(s, 16)
    kron(3 * BLK, True, t)

    for x in range(G):
        out_ref[:, x * PLANE:(x + 1) * PLANE] = t[4 * x:4 * x + 4, :]


def hamiltonian(orbitals, potential, magic_taps, kinetic_taps):
    count = orbitals.shape[0]
    rows = count * G
    vmem = pl.BlockSpec(memory_space=pltpu.VMEM)
    smem = pl.BlockSpec(memory_space=pltpu.SMEM)
    return pl.pallas_call(
        h_kernel,
        out_shape=jax.ShapeDtypeStruct(orbitals.shape, F32),
        in_specs=[smem, smem, vmem, vmem],
        out_specs=vmem,
        scratch_shapes=[
            pltpu.VMEM((rows, PLANE), F32),
            pltpu.VMEM((rows, PLANE), F32),
            pltpu.VMEM((G, BLK), F32),
            pltpu.VMEM((G, BLK), F32),
            pltpu.VMEM((G, BLK), F32),
            pltpu.VMEM((PLANE, BLK), BF16),
            pltpu.VMEM((PLANE, BLK), BF16),
            pltpu.VMEM((6 * rows, PLANE), BF16),
            pltpu.VMEM((6 * rows, 256), F32),
            pltpu.VMEM((rows, 2 * PLANE), BF16),
            pltpu.VMEM((2 * rows, rows), BF16),
        ],
        compiler_params=pltpu.CompilerParams(vmem_limit_bytes=36 * 1024 * 1024),
        cost_estimate=pl.CostEstimate(
            flops=24_000_000_000, transcendentals=0, bytes_accessed=12 * orbitals.size
        ),
        name="hamiltonian",
    )(magic_taps, kinetic_taps, orbitals, potential.reshape(G, PLANE))


def exchange(pieces):
    return lax.all_to_all(pieces, COEF, split_axis=0, concat_axis=0, tiled=True)


def to_cols(block):
    pieces = block.reshape(block.shape[0], NSPLIT, -1).transpose(1, 0, 2)
    return exchange(pieces)


def step_x(pieces, step):
    return lax.ppermute(pieces, "x", [(i, (i + step) % 4) for i in range(4)])


def swap_core(value):
    return lax.ppermute(value, "core", [(0, 1), (1, 0)])


def rows_of(ref, scratch, start):
    count = ref.shape[0]
    for s in range(count):
        scratch[start + 4 * s:start + 4 * s + 4, :] = ref[s]


NT = (((1,), (1,)), ((), ()))


def add_up(out, place, total):
    @pl.when(pl.program_id(0) == 0)
    def _():
        out[:, place] = total

    @pl.when(pl.program_id(0) > 0)
    def _():
        out[:, place] += total


def margin_terms(panels, psi, hsp_ref, high_ref, low_ref):
    at = 0
    for ref in panels:
        rows_of(ref, psi, at)
        at += 4 * ref.shape[0]
    cols = hsp_ref.shape[0] // 2
    p_hi, p_lo = split_bf16(psi[...])
    high_ref[...] = p_hi
    low_ref[...] = p_lo
    both = lax.dot_general(hsp_ref[...], p_hi, NT, preferred_element_type=F32)
    cross = lax.dot_general(hsp_ref[0:cols, :], p_lo, NT, preferred_element_type=F32)
    return (both[0:cols] + both[cols:] + cross) * (1.0 / NC)


def near_kernel(*refs):
    panels, (own_ref, swap_ref, out_ref, high_ref, low_ref, hsp_ref, psi, hps) = refs[:-8], refs[-8:]
    cols = hps.shape[0]
    rows_of(own_ref, hps, 0)
    rows_of(swap_ref, hps, cols // 2)
    high, low = split_bf16(hps[...])
    hsp_ref[0:cols, :] = high
    hsp_ref[cols:, :] = low
    add_up(out_ref, slice(None), margin_terms(panels, psi, hsp_ref, high_ref, low_ref))


def far_kernel(near_ref, hsp_ref, *refs):
    panels, (out_ref, high_ref, low_ref, psi) = refs[:-4], refs[-4:]
    start = near_ref.shape[1]

    @pl.when(pl.program_id(0) == 0)
    def _():
        out_ref[:, 0:start] = near_ref[...]

    add_up(out_ref, slice(start, None), margin_terms(panels, psi, hsp_ref, high_ref, low_ref))


def chunk_spec(array, chunk):
    return pl.BlockSpec((*array.shape[:-1], chunk), lambda k: (0,) * (len(array.shape) - 1) + (k,))


def in_hbm(rows, width):
    return pltpu.MemorySpace.HBM((rows, width), BF16)


def near_outs(rows, cols):
    return lambda w: [in_hbm(rows, w)] * 2 + [jax.ShapeDtypeStruct((2 * cols, w), BF16)]


def far_outs(rows):
    return lambda w: [jax.ShapeDtypeStruct((rows, w), BF16)] * 2


def margin_call(kernel, rows, cols, out_cols, extra, whole, arrays, outs, name):
    width = arrays[-1].shape[-1]
    return pl.pallas_call(
        kernel,
        grid=(width // CHUNK,),
        out_shape=[jax.ShapeDtypeStruct((cols, out_cols), F32)] + outs(width),
        in_specs=[pl.BlockSpec(v.shape, lambda k: (0, 0)) for v in whole]
        + [chunk_spec(v, CHUNK) for v in arrays],
        out_specs=[pl.BlockSpec((cols, out_cols), lambda k: (0, 0))]
        + [chunk_spec(v, CHUNK) for v in outs(width)],
        scratch_shapes=[pltpu.VMEM((rows, CHUNK), F32)] + extra,
        cost_estimate=pl.CostEstimate(
            flops=6 * rows * cols * width, transcendentals=0,
            bytes_accessed=4 * (2 * rows + 2 * cols) * width,
        ),
        compiler_params=pltpu.CompilerParams(vmem_limit_bytes=24 * 1024 * 1024),
        name=name,
    )(*whole, *arrays)


def rows_in(panels):
    return sum(4 * v.shape[0] for v in panels)


def near_part(panels, own, swap):
    rows, cols = rows_in(panels), rows_in([own, swap])
    return margin_call(
        near_kernel, rows, cols, rows, [pltpu.VMEM((cols, CHUNK), F32)], [],
        [*panels, own, swap], near_outs(rows, cols), "near_part",
    )


def far_part(near, hsp, panels):
    rows, cols = rows_in(panels), near.shape[0]
    return margin_call(
        far_kernel, rows, cols, near.shape[1] + rows, [], [near], [hsp, *panels], far_outs(rows), "far_part",
    )


def rotate_kernel(margin_ref, *refs):
    halves, (base_ref, mine_ref, other_ref, turn, res) = refs[:-5], refs[-5:]
    cols = margin_ref.shape[0]

    @pl.when(pl.program_id(0) == 0)
    def _():
        high, low = split_bf16(margin_ref[...])
        turn[0:cols, :] = high
        turn[cols:, :] = low

    at = 0
    total = None
    for high_ref, low_ref in zip(halves[::2], halves[1::2]):
        upto = at + high_ref.shape[0]
        both = jnp.dot(turn[:, at:upto], high_ref[...], preferred_element_type=F32)
        low = jnp.dot(turn[0:cols, at:upto], low_ref[...], preferred_element_type=F32)
        value = both[0:cols] + both[cols:] + low
        total = value if total is None else total + value
        at = upto
    res[...] = total
    for s in range(mine_ref.shape[0]):
        mine_ref[s] = base_ref[s] - res[4 * s:4 * s + 4, :]
        other_ref[s] = res[cols // 2 + 4 * s:cols // 2 + 4 * s + 4, :]


def rotated(margin, halves, base):
    cols, rows = margin.shape
    width = base.shape[2]
    shape = jax.ShapeDtypeStruct(base.shape, F32)
    return pl.pallas_call(
        rotate_kernel,
        grid=(width // WIDE,),
        out_shape=[shape, shape],
        in_specs=[pl.BlockSpec(margin.shape, lambda k: (0, 0))]
        + [chunk_spec(v, WIDE) for v in (*halves, base)],
        out_specs=[chunk_spec(base, WIDE)] * 2,
        scratch_shapes=[pltpu.VMEM((2 * cols, rows), BF16), pltpu.VMEM((cols, WIDE), F32)],
        cost_estimate=pl.CostEstimate(
            flops=6 * rows * cols * width, transcendentals=0,
            bytes_accessed=4 * (rows + 2 * cols) * width,
        ),
        compiler_params=pltpu.CompilerParams(vmem_limit_bytes=48 * 1024 * 1024),
        name="rotated",
    )(margin, *halves, base)


def shards(orbitals, potential, magic_taps, kinetic_taps):
    own = to_cols(orbitals)
    hpsi = hamiltonian(orbitals, potential, magic_taps, kinetic_taps)
    own, _ = lax.optimization_barrier((own, hpsi))
    left, right = step_x(own, 1), step_x(own, -1)
    hpsi_cols = to_cols(hpsi)
    half = NSPLIT // 2
    far_a, far_b = step_x(left[:half], 1), step_x(right[half:], -1)
    hpsi_swap = swap_core(hpsi_cols)
    near, *near_halves, hsp = near_part([own, left, right], hpsi_cols, hpsi_swap)
    part, *far_halves = far_part(near, hsp, [far_a, far_b])
    mine = jnp.sum(exchange(part.reshape(NSPLIT, -1, part.shape[1])), axis=0)
    margin = exchange(jnp.broadcast_to(mine[None], (NSPLIT, *mine.shape))).reshape(part.shape)
    grad_mine, grad_other = rotated(margin, near_halves + far_halves, hpsi_cols)
    grad_cols = grad_mine - swap_core(grad_other)
    back = exchange(grad_cols)
    return back.transpose(1, 0, 2).reshape(orbitals.shape)


def solution(mesh):
    fine = Mesh(mesh.devices.reshape(SPLIT), NAMES)
    placed = (P(NAMES, None), P(), P(), P())
    return jax.shard_map(
        shards, mesh=fine, in_specs=placed, out_specs=P(NAMES, None), check_vma=False
    )
```

```python
import functools

import jax
import jax.numpy as jnp
from jax import lax
from jax.experimental import pallas as pl
from jax.experimental.pallas import tpu as pltpu
from jax.sharding import Mesh, PartitionSpec as P

G = 48
NC = 110592
SPLIT = (4, 2, 4, 2, 4)
NAMES = ("x", "zl", "y", "core", "zh")
COEF = ("y", "zl", "zh")
NSPLIT = 32
CHUNK = 1152
WIDE = 1152
PLANE = G * G
BLK = 16 * G
F32 = jnp.float32
BF16 = jnp.bfloat16


def split_bf16(value):
    high = value.astype(BF16)
    return high, (value - high.astype(F32)).astype(BF16)


def pick_taps(taps_ref, count, offset):
    out = jnp.zeros(offset.shape, F32)
    for k in range(count):
        out = jnp.where(offset == k, taps_ref[k], out)
    return out


def wrap(offset):
    return jnp.where(offset < 0, offset + G, jnp.where(offset >= G, offset - G, offset))


def ints(shape, dim):
    return lax.broadcasted_iota(jnp.int32, shape, dim)


def div_g(value):
    return (value * 1366) >> 16


def x_matrix(taps_ref, count, rows, transposed):
    shape = (rows, rows)
    r, c = ints(shape, 0), ints(shape, 1)
    gap = (r >> 2) - (c >> 2) if transposed else (c >> 2) - (r >> 2)
    offset = wrap(gap + (count - 1) // 2)
    return jnp.where((r & 3) == (c & 3), pick_taps(taps_ref, count, offset), 0.0)


def z_table(taps_ref, count, transposed):
    shape = (G, BLK)
    lane = ints(shape, 1)
    z_out = lane - G * div_g(lane)
    z_in = ints(shape, 0)
    gap = z_out - z_in if transposed else z_in - z_out
    return pick_taps(taps_ref, count, wrap(gap + (count - 1) // 2))


def y_table(taps_ref, count, reach, transposed):
    shape = (16 + 2 * reach, BLK)
    gap = ints(shape, 0) - reach - div_g(ints(shape, 1))
    if transposed:
        gap = -gap
    return pick_taps(taps_ref, count, gap + (count - 1) // 2)


def h_kernel(magic_ref, kinetic_ref, psi_ref, pot_ref, out_ref,
             s, t, zt, zt2, yt, w_hi, w_lo, lhs, prod, pad, xm):
    rows = s.shape[0]
    n_magic, n_kin = magic_ref.shape[0], kinetic_ref.shape[0]

    def fill_weights(depth, with_identity):
        def body(j, carry):
            value = zt[...] * yt[pl.ds(j, 1), :]
            if with_identity:
                lane = ints((1, BLK), 1)
                same = jnp.where(div_g(lane) == j - 16, 1.0, 0.0).astype(F32)
                value = value + zt2[...] * same
            high, low = split_bf16(value)
            at = pl.multiple_of(j * G, G)
            w_hi[pl.ds(at, G), :] = high
            w_lo[pl.ds(at, G), :] = low
            return carry
        lax.fori_loop(0, depth, body, 0)

    def fill_lhs(source, reach):
        edge = reach * G
        width = (16 + 2 * reach) * G
        for part in range(2):
            pad[:, 0:PLANE] = split_bf16(source[...])[part]
            pad[:, PLANE:2 * PLANE] = pad[:, 0:PLANE]
            for n in range(3):
                start = (BLK * n - edge) % PLANE
                lhs[pl.ds((3 * part + n) * rows, rows), 0:width] = pad[:, start:start + width]

    def kron(width, accumulate, target):
        def body(nt, carry):
            at = pl.multiple_of(nt * 256, 256)
            cols = pl.ds(at, 256)
            prod[...] = jnp.dot(lhs[:, 0:width], w_hi[0:width, cols], preferred_element_type=F32)
            low = jnp.dot(lhs[0:3 * rows, 0:width], w_lo[0:width, cols], preferred_element_type=F32)
            for n in range(3):
                value = (prod[n * rows:(n + 1) * rows, :] + prod[(3 + n) * rows:(4 + n) * rows, :]
                         + low[n * rows:(n + 1) * rows, :])
                place = pl.ds(pl.multiple_of(BLK * n + nt * 256, 256), 256)
                if accumulate:
                    value = value + target[:, place]
                target[:, place] = value
            return carry
        lax.fori_loop(0, 3, body, 0)

    def along_x(matrix, source, finish):
        high, low = split_bf16(matrix)
        xm[0:rows, :] = high
        xm[rows:, :] = low

        def body(nt, carry):
            cols = pl.ds(pl.multiple_of(nt * 256, 256), 256)
            b_hi, b_lo = split_bf16(source[:, cols])
            both = jnp.dot(xm[...], b_hi, preferred_element_type=F32)
            low = jnp.dot(xm[0:rows, :], b_lo, preferred_element_type=F32)
            finish(cols, both[0:rows] + both[rows:] + low)
            return carry
        lax.fori_loop(0, PLANE // 256, body, 0)

    for x in range(G):
        s[4 * x:4 * x + 4, :] = psi_ref[:, x * PLANE:(x + 1) * PLANE]

    zt[...] = z_table(magic_ref, n_magic, False)
    yt[0:32, :] = y_table(magic_ref, n_magic, 8, False)
    fill_weights(32, False)
    fill_lhs(s, 8)
    kron(2 * BLK, False, t)

    def magic_and_potential(cols, value):
        pot = pot_ref[:, cols]
        t[:, cols] = value * jnp.broadcast_to(pot[:, None, :], (G, 4, 256)).reshape(rows, 256)

    along_x(x_matrix(magic_ref, n_magic, rows, False), t, magic_and_potential)

    def keep(cols, value):
        t[:, cols] = value

    along_x(x_matrix(magic_ref, n_magic, rows, True), t, keep)

    zt[...] = z_table(magic_ref, n_magic, True)
    yt[0:32, :] = y_table(magic_ref, n_magic, 8, True)
    fill_weights(32, False)
    fill_lhs(t, 8)

    def start_sum(cols, value):
        t[:, cols] = value

    along_x(x_matrix(kinetic_ref, n_kin, rows, False), s, start_sum)
    kron(2 * BLK, True, t)

    shape = (G, BLK)
    lane = ints(shape, 1)
    zt[...] = jnp.where(lane - G * div_g(lane) == ints(shape, 0), 1.0, 0.0).astype(F32)
    zt2[...] = z_table(kinetic_ref, n_kin, False)
    yt[...] = y_table(kinetic_ref, n_kin, 16, False)
    fill_weights(48, True)
    fill_lhs(s, 16)
    kron(3 * BLK, True, t)

    for x in range(G):
        out_ref[:, x * PLANE:(x + 1) * PLANE] = t[4 * x:4 * x + 4, :]


def hamiltonian(orbitals, potential, magic_taps, kinetic_taps):
    count = orbitals.shape[0]
    rows = count * G
    vmem = pl.BlockSpec(memory_space=pltpu.VMEM)
    smem = pl.BlockSpec(memory_space=pltpu.SMEM)
    return pl.pallas_call(
        h_kernel,
        out_shape=jax.ShapeDtypeStruct(orbitals.shape, F32),
        in_specs=[smem, smem, vmem, vmem],
        out_specs=vmem,
        scratch_shapes=[
            pltpu.VMEM((rows, PLANE), F32),
            pltpu.VMEM((rows, PLANE), F32),
            pltpu.VMEM((G, BLK), F32),
            pltpu.VMEM((G, BLK), F32),
            pltpu.VMEM((G, BLK), F32),
            pltpu.VMEM((PLANE, BLK), BF16),
            pltpu.VMEM((PLANE, BLK), BF16),
            pltpu.VMEM((6 * rows, PLANE), BF16),
            pltpu.VMEM((6 * rows, 256), F32),
            pltpu.VMEM((rows, 2 * PLANE), BF16),
            pltpu.VMEM((2 * rows, rows), BF16),
        ],
        compiler_params=pltpu.CompilerParams(vmem_limit_bytes=36 * 1024 * 1024),
        cost_estimate=pl.CostEstimate(
            flops=24_000_000_000, transcendentals=0, bytes_accessed=12 * orbitals.size
        ),
        name="hamiltonian",
    )(magic_taps, kinetic_taps, orbitals, potential.reshape(G, PLANE))


def exchange(pieces):
    return lax.all_to_all(pieces, COEF, split_axis=0, concat_axis=0, tiled=True)


def to_cols(block):
    pieces = block.reshape(block.shape[0], NSPLIT, -1).transpose(1, 0, 2)
    return exchange(pieces)


def step_x(pieces, step):
    return lax.ppermute(pieces, "x", [(i, (i + step) % 4) for i in range(4)])


def swap_core(value):
    return lax.ppermute(value, "core", [(0, 1), (1, 0)])


def rows_of(ref, scratch, start):
    count = ref.shape[0]
    for s in range(count):
        scratch[start + 4 * s:start + 4 * s + 4, :] = ref[s]


NT = (((1,), (1,)), ((), ()))


def add_up(out, place, total):
    @pl.when(pl.program_id(0) == 0)
    def _():
        out[:, place] = total

    @pl.when(pl.program_id(0) > 0)
    def _():
        out[:, place] += total


def margin_terms(panels, psi, hsp_ref, high_ref, low_ref):
    at = 0
    for ref in panels:
        rows_of(ref, psi, at)
        at += 4 * ref.shape[0]
    cols = hsp_ref.shape[0] // 2
    p_hi, p_lo = split_bf16(psi[...])
    high_ref[...] = p_hi
    low_ref[...] = p_lo
    both = lax.dot_general(hsp_ref[...], p_hi, NT, preferred_element_type=F32)
    cross = lax.dot_general(hsp_ref[0:cols, :], p_lo, NT, preferred_element_type=F32)
    return (both[0:cols] + both[cols:] + cross) * (1.0 / NC)


def near_kernel(*refs):
    panels, (own_ref, swap_ref, out_ref, high_ref, low_ref, hsp_ref, psi, hps) = refs[:-8], refs[-8:]
    cols = hps.shape[0]
    rows_of(own_ref, hps, 0)
    rows_of(swap_ref, hps, cols // 2)
    high, low = split_bf16(hps[...])
    hsp_ref[0:cols, :] = high
    hsp_ref[cols:, :] = low
    add_up(out_ref, slice(None), margin_terms(panels, psi, hsp_ref, high_ref, low_ref))


def far_kernel(near_ref, hsp_ref, *refs):
    panels, (out_ref, high_ref, low_ref, psi) = refs[:-4], refs[-4:]
    start = near_ref.shape[1]

    @pl.when(pl.program_id(0) == 0)
    def _():
        out_ref[:, 0:start] = near_ref[...]

    add_up(out_ref, slice(start, None), margin_terms(panels, psi, hsp_ref, high_ref, low_ref))


def chunk_spec(array, chunk):
    return pl.BlockSpec((*array.shape[:-1], chunk), lambda k: (0,) * (len(array.shape) - 1) + (k,))


def in_hbm(rows, width):
    return pltpu.MemorySpace.HBM((rows, width), BF16)


def near_outs(rows, cols):
    return lambda w: [in_hbm(rows, w)] * 2 + [jax.ShapeDtypeStruct((2 * cols, w), BF16)]


def far_outs(rows):
    return lambda w: [jax.ShapeDtypeStruct((rows, w), BF16)] * 2


def margin_call(kernel, rows, cols, out_cols, extra, whole, arrays, outs, name):
    width = arrays[-1].shape[-1]
    return pl.pallas_call(
        kernel,
        grid=(width // CHUNK,),
        out_shape=[jax.ShapeDtypeStruct((cols, out_cols), F32)] + outs(width),
        in_specs=[pl.BlockSpec(v.shape, lambda k: (0, 0)) for v in whole]
        + [chunk_spec(v, CHUNK) for v in arrays],
        out_specs=[pl.BlockSpec((cols, out_cols), lambda k: (0, 0))]
        + [chunk_spec(v, CHUNK) for v in outs(width)],
        scratch_shapes=[pltpu.VMEM((rows, CHUNK), F32)] + extra,
        cost_estimate=pl.CostEstimate(
            flops=6 * rows * cols * width, transcendentals=0,
            bytes_accessed=4 * (2 * rows + 2 * cols) * width,
        ),
        compiler_params=pltpu.CompilerParams(vmem_limit_bytes=24 * 1024 * 1024),
        name=name,
    )(*whole, *arrays)


def rows_in(panels):
    return sum(4 * v.shape[0] for v in panels)


def near_part(panels, own, swap):
    rows, cols = rows_in(panels), rows_in([own, swap])
    return margin_call(
        near_kernel, rows, cols, rows, [pltpu.VMEM((cols, CHUNK), F32)], [],
        [*panels, own, swap], near_outs(rows, cols), "near_part",
    )


def far_part(near, hsp, panels):
    rows, cols = rows_in(panels), near.shape[0]
    return margin_call(
        far_kernel, rows, cols, near.shape[1] + rows, [], [near], [hsp, *panels], far_outs(rows), "far_part",
    )


def rotate_kernel(count, margin_ref, *refs):
    halves, bases, (out_ref, turn, res) = refs[:count], refs[count:-3], refs[-3:]
    cols = margin_ref.shape[0]

    @pl.when(pl.program_id(0) == 0)
    def _():
        high, low = split_bf16(margin_ref[...])
        turn[0:cols, :] = high
        turn[cols:, :] = low

    at = 0
    total = None
    for high_ref, low_ref in zip(halves[::2], halves[1::2]):
        upto = at + high_ref.shape[0]
        both = jnp.dot(turn[:, at:upto], high_ref[...], preferred_element_type=F32)
        low = jnp.dot(turn[0:cols, at:upto], low_ref[...], preferred_element_type=F32)
        value = both[0:cols] + both[cols:] + low
        total = value if total is None else total + value
        at = upto
    res[...] = total
    for s in range(out_ref.shape[0]):
        value = res[4 * s:4 * s + 4, :]
        out_ref[s] = bases[0][s] - value if bases else value


def rotated(margin, side, halves, *bases):
    cols, rows = margin.shape[0] // 2, margin.shape[1]
    width = halves[0].shape[1]
    out = jax.ShapeDtypeStruct((cols // 4, 4, width), F32)
    return pl.pallas_call(
        functools.partial(rotate_kernel, len(halves)),
        grid=(width // WIDE,),
        out_shape=out,
        in_specs=[pl.BlockSpec((cols, rows), lambda k: (side, 0))]
        + [chunk_spec(v, WIDE) for v in (*halves, *bases)],
        out_specs=chunk_spec(out, WIDE),
        scratch_shapes=[pltpu.VMEM((2 * cols, rows), BF16), pltpu.VMEM((cols, WIDE), F32)],
        cost_estimate=pl.CostEstimate(
            flops=6 * rows * cols * width, transcendentals=0,
            bytes_accessed=4 * (rows + 2 * cols) * width,
        ),
        compiler_params=pltpu.CompilerParams(vmem_limit_bytes=48 * 1024 * 1024),
        name="rotated",
    )(margin, *halves, *bases)


def shards(orbitals, potential, magic_taps, kinetic_taps):
    own = to_cols(orbitals)
    hpsi = hamiltonian(orbitals, potential, magic_taps, kinetic_taps)
    own, _ = lax.optimization_barrier((own, hpsi))
    left, right = step_x(own, 1), step_x(own, -1)
    hpsi_cols = to_cols(hpsi)
    half = NSPLIT // 2
    far_a, far_b = step_x(left[:half], 1), step_x(right[half:], -1)
    hpsi_swap = swap_core(hpsi_cols)
    near, *near_halves, hsp = near_part([own, left, right], hpsi_cols, hpsi_swap)
    part, *far_halves = far_part(near, hsp, [far_a, far_b])
    mine = jnp.sum(exchange(part.reshape(NSPLIT, -1, part.shape[1])), axis=0)
    margin = exchange(jnp.broadcast_to(mine[None], (NSPLIT, *mine.shape))).reshape(part.shape)
    halves = near_halves + far_halves
    from_other = swap_core(rotated(margin, 1, halves))
    grad_cols = rotated(margin, 0, halves, hpsi_cols) - from_other
    back = exchange(grad_cols)
    return back.transpose(1, 0, 2).reshape(orbitals.shape)


def solution(mesh):
    fine = Mesh(mesh.devices.reshape(SPLIT), NAMES)
    placed = (P(NAMES, None), P(), P(), P())
    return jax.shard_map(
        shards, mesh=fine, in_specs=placed, out_specs=P(NAMES, None), check_vma=False
    )
```

```python
import functools

import jax
import jax.numpy as jnp
from jax import lax
from jax.experimental import pallas as pl
from jax.experimental.pallas import tpu as pltpu
from jax.sharding import Mesh, PartitionSpec as P

G = 48
NC = 110592
SPLIT = (4, 2, 4, 2, 4)
NAMES = ("x", "zl", "y", "core", "zh")
COEF = ("y", "zl", "zh")
NSPLIT = 32
CHUNK = 1152
WIDE = 1152
PLANE = G * G
BLK = 16 * G
F32 = jnp.float32
BF16 = jnp.bfloat16


def split_bf16(value):
    high = value.astype(BF16)
    return high, (value - high.astype(F32)).astype(BF16)


def pick_taps(taps_ref, count, offset):
    out = jnp.zeros(offset.shape, F32)
    for k in range(count):
        out = jnp.where(offset == k, taps_ref[k], out)
    return out


def wrap(offset):
    return jnp.where(offset < 0, offset + G, jnp.where(offset >= G, offset - G, offset))


def ints(shape, dim):
    return lax.broadcasted_iota(jnp.int32, shape, dim)


def div_g(value):
    return (value * 1366) >> 16


def x_matrix(taps_ref, count, rows, transposed):
    shape = (rows, rows)
    r, c = ints(shape, 0), ints(shape, 1)
    gap = (r >> 2) - (c >> 2) if transposed else (c >> 2) - (r >> 2)
    offset = wrap(gap + (count - 1) // 2)
    return jnp.where((r & 3) == (c & 3), pick_taps(taps_ref, count, offset), 0.0)


def z_table(taps_ref, count, transposed):
    shape = (G, BLK)
    lane = ints(shape, 1)
    z_out = lane - G * div_g(lane)
    z_in = ints(shape, 0)
    gap = z_out - z_in if transposed else z_in - z_out
    return pick_taps(taps_ref, count, wrap(gap + (count - 1) // 2))


def y_table(taps_ref, count, reach, transposed):
    shape = (16 + 2 * reach, BLK)
    gap = ints(shape, 0) - reach - div_g(ints(shape, 1))
    if transposed:
        gap = -gap
    return pick_taps(taps_ref, count, gap + (count - 1) // 2)


def h_kernel(magic_ref, kinetic_ref, psi_ref, pot_ref, out_ref,
             s, t, zt, zt2, yt, w_hi, w_lo, lhs, prod, pad, xm):
    rows = s.shape[0]
    n_magic, n_kin = magic_ref.shape[0], kinetic_ref.shape[0]

    def fill_weights(depth, with_identity):
        def body(j, carry):
            value = zt[...] * yt[pl.ds(j, 1), :]
            if with_identity:
                lane = ints((1, BLK), 1)
                same = jnp.where(div_g(lane) == j - 16, 1.0, 0.0).astype(F32)
                value = value + zt2[...] * same
            high, low = split_bf16(value)
            at = pl.multiple_of(j * G, G)
            w_hi[pl.ds(at, G), :] = high
            w_lo[pl.ds(at, G), :] = low
            return carry
        lax.fori_loop(0, depth, body, 0)

    def fill_lhs(source, reach):
        edge = reach * G
        width = (16 + 2 * reach) * G
        for part in range(2):
            pad[:, 0:PLANE] = split_bf16(source[...])[part]
            pad[:, PLANE:2 * PLANE] = pad[:, 0:PLANE]
            for n in range(3):
                start = (BLK * n - edge) % PLANE
                lhs[pl.ds((3 * part + n) * rows, rows), 0:width] = pad[:, start:start + width]

    def kron(width, accumulate, target):
        def body(nt, carry):
            at = pl.multiple_of(nt * 256, 256)
            cols = pl.ds(at, 256)
            prod[...] = jnp.dot(lhs[:, 0:width], w_hi[0:width, cols], preferred_element_type=F32)
            low = jnp.dot(lhs[0:3 * rows, 0:width], w_lo[0:width, cols], preferred_element_type=F32)
            for n in range(3):
                value = (prod[n * rows:(n + 1) * rows, :] + prod[(3 + n) * rows:(4 + n) * rows, :]
                         + low[n * rows:(n + 1) * rows, :])
                place = pl.ds(pl.multiple_of(BLK * n + nt * 256, 256), 256)
                if accumulate:
                    value = value + target[:, place]
                target[:, place] = value
            return carry
        lax.fori_loop(0, 3, body, 0)

    def along_x(matrix, source, finish):
        high, low = split_bf16(matrix)
        xm[0:rows, :] = high
        xm[rows:, :] = low

        def body(nt, carry):
            cols = pl.ds(pl.multiple_of(nt * 256, 256), 256)
            b_hi, b_lo = split_bf16(source[:, cols])
            both = jnp.dot(xm[...], b_hi, preferred_element_type=F32)
            low = jnp.dot(xm[0:rows, :], b_lo, preferred_element_type=F32)
            finish(cols, both[0:rows] + both[rows:] + low)
            return carry
        lax.fori_loop(0, PLANE // 256, body, 0)

    for x in range(G):
        s[4 * x:4 * x + 4, :] = psi_ref[:, x * PLANE:(x + 1) * PLANE]

    zt[...] = z_table(magic_ref, n_magic, False)
    yt[0:32, :] = y_table(magic_ref, n_magic, 8, False)
    fill_weights(32, False)
    fill_lhs(s, 8)
    kron(2 * BLK, False, t)

    def magic_and_potential(cols, value):
        pot = pot_ref[:, cols]
        t[:, cols] = value * jnp.broadcast_to(pot[:, None, :], (G, 4, 256)).reshape(rows, 256)

    along_x(x_matrix(magic_ref, n_magic, rows, False), t, magic_and_potential)

    def keep(cols, value):
        t[:, cols] = value

    along_x(x_matrix(magic_ref, n_magic, rows, True), t, keep)

    zt[...] = z_table(magic_ref, n_magic, True)
    yt[0:32, :] = y_table(magic_ref, n_magic, 8, True)
    fill_weights(32, False)
    fill_lhs(t, 8)

    def start_sum(cols, value):
        t[:, cols] = value

    along_x(x_matrix(kinetic_ref, n_kin, rows, False), s, start_sum)
    kron(2 * BLK, True, t)

    shape = (G, BLK)
    lane = ints(shape, 1)
    zt[...] = jnp.where(lane - G * div_g(lane) == ints(shape, 0), 1.0, 0.0).astype(F32)
    zt2[...] = z_table(kinetic_ref, n_kin, False)
    yt[...] = y_table(kinetic_ref, n_kin, 16, False)
    fill_weights(48, True)
    fill_lhs(s, 16)
    kron(3 * BLK, True, t)

    for x in range(G):
        out_ref[:, x * PLANE:(x + 1) * PLANE] = t[4 * x:4 * x + 4, :]


def hamiltonian(orbitals, potential, magic_taps, kinetic_taps):
    count = orbitals.shape[0]
    rows = count * G
    vmem = pl.BlockSpec(memory_space=pltpu.VMEM)
    smem = pl.BlockSpec(memory_space=pltpu.SMEM)
    return pl.pallas_call(
        h_kernel,
        out_shape=jax.ShapeDtypeStruct(orbitals.shape, F32),
        in_specs=[smem, smem, vmem, vmem],
        out_specs=vmem,
        scratch_shapes=[
            pltpu.VMEM((rows, PLANE), F32),
            pltpu.VMEM((rows, PLANE), F32),
            pltpu.VMEM((G, BLK), F32),
            pltpu.VMEM((G, BLK), F32),
            pltpu.VMEM((G, BLK), F32),
            pltpu.VMEM((PLANE, BLK), BF16),
            pltpu.VMEM((PLANE, BLK), BF16),
            pltpu.VMEM((6 * rows, PLANE), BF16),
            pltpu.VMEM((6 * rows, 256), F32),
            pltpu.VMEM((rows, 2 * PLANE), BF16),
            pltpu.VMEM((2 * rows, rows), BF16),
        ],
        compiler_params=pltpu.CompilerParams(vmem_limit_bytes=36 * 1024 * 1024),
        cost_estimate=pl.CostEstimate(
            flops=24_000_000_000, transcendentals=0, bytes_accessed=12 * orbitals.size
        ),
        name="hamiltonian",
    )(magic_taps, kinetic_taps, orbitals, potential.reshape(G, PLANE))


def exchange(pieces):
    return lax.all_to_all(pieces, COEF, split_axis=0, concat_axis=0, tiled=True)


def spread(value, axes, count):
    copies = jnp.broadcast_to(value[None], (count, *value.shape))
    return lax.all_to_all(copies, axes, split_axis=0, concat_axis=0, tiled=True).reshape(
        -1, value.shape[1]
    )


def to_cols(block):
    pieces = block.reshape(block.shape[0], NSPLIT, -1).transpose(1, 0, 2)
    return exchange(pieces)


def step_x(pieces, step):
    return lax.ppermute(pieces, "x", [(i, (i + step) % 4) for i in range(4)])


def swap_core(value):
    return lax.ppermute(value, "core", [(0, 1), (1, 0)])


def rows_of(ref, scratch, start):
    count = ref.shape[0]
    for s in range(count):
        scratch[start + 4 * s:start + 4 * s + 4, :] = ref[s]


NT = (((1,), (1,)), ((), ()))


def add_up(out, place, total):
    @pl.when(pl.program_id(0) == 0)
    def _():
        out[:, place] = total

    @pl.when(pl.program_id(0) > 0)
    def _():
        out[:, place] += total


def margin_terms(panels, psi, hsp_ref, high_ref, low_ref):
    at = 0
    for ref in panels:
        rows_of(ref, psi, at)
        at += 4 * ref.shape[0]
    cols = hsp_ref.shape[0] // 2
    p_hi, p_lo = split_bf16(psi[...])
    high_ref[...] = p_hi
    low_ref[...] = p_lo
    both = lax.dot_general(hsp_ref[...], p_hi, NT, preferred_element_type=F32)
    cross = lax.dot_general(hsp_ref[0:cols, :], p_lo, NT, preferred_element_type=F32)
    return (both[0:cols] + both[cols:] + cross) * (1.0 / NC)


def near_kernel(*refs):
    panels, (own_ref, swap_ref, out_ref, high_ref, low_ref, hsp_ref, psi, hps) = refs[:-8], refs[-8:]
    cols = hps.shape[0]
    rows_of(own_ref, hps, 0)
    rows_of(swap_ref, hps, cols // 2)
    high, low = split_bf16(hps[...])
    hsp_ref[0:cols, :] = high
    hsp_ref[cols:, :] = low
    add_up(out_ref, slice(None), margin_terms(panels, psi, hsp_ref, high_ref, low_ref))


def far_kernel(near_ref, hsp_ref, *refs):
    panels, (out_ref, high_ref, low_ref, psi) = refs[:-4], refs[-4:]
    start = near_ref.shape[1]

    @pl.when(pl.program_id(0) == 0)
    def _():
        out_ref[:, 0:start] = near_ref[...]

    add_up(out_ref, slice(start, None), margin_terms(panels, psi, hsp_ref, high_ref, low_ref))


def chunk_spec(array, chunk):
    return pl.BlockSpec((*array.shape[:-1], chunk), lambda k: (0,) * (len(array.shape) - 1) + (k,))


def in_hbm(rows, width):
    return pltpu.MemorySpace.HBM((rows, width), BF16)


def near_outs(rows, cols):
    return lambda w: [in_hbm(rows, w)] * 2 + [jax.ShapeDtypeStruct((2 * cols, w), BF16)]


def far_outs(rows):
    return lambda w: [jax.ShapeDtypeStruct((rows, w), BF16)] * 2


def margin_call(kernel, rows, cols, out_cols, extra, whole, arrays, outs, name):
    width = arrays[-1].shape[-1]
    return pl.pallas_call(
        kernel,
        grid=(width // CHUNK,),
        out_shape=[jax.ShapeDtypeStruct((cols, out_cols), F32)] + outs(width),
        in_specs=[pl.BlockSpec(v.shape, lambda k: (0, 0)) for v in whole]
        + [chunk_spec(v, CHUNK) for v in arrays],
        out_specs=[pl.BlockSpec((cols, out_cols), lambda k: (0, 0))]
        + [chunk_spec(v, CHUNK) for v in outs(width)],
        scratch_shapes=[pltpu.VMEM((rows, CHUNK), F32)] + extra,
        cost_estimate=pl.CostEstimate(
            flops=6 * rows * cols * width, transcendentals=0,
            bytes_accessed=4 * (2 * rows + 2 * cols) * width,
        ),
        compiler_params=pltpu.CompilerParams(vmem_limit_bytes=24 * 1024 * 1024),
        name=name,
    )(*whole, *arrays)


def rows_in(panels):
    return sum(4 * v.shape[0] for v in panels)


def near_part(panels, own, swap):
    rows, cols = rows_in(panels), rows_in([own, swap])
    return margin_call(
        near_kernel, rows, cols, rows, [pltpu.VMEM((cols, CHUNK), F32)], [],
        [*panels, own, swap], near_outs(rows, cols), "near_part",
    )


def far_part(near, hsp, panels):
    rows, cols = rows_in(panels), near.shape[0]
    return margin_call(
        far_kernel, rows, cols, near.shape[1] + rows, [], [near], [hsp, *panels], far_outs(rows), "far_part",
    )


def rotate_kernel(count, margin_ref, *refs):
    halves, bases, (out_ref, turn, res) = refs[:count], refs[count:-3], refs[-3:]
    cols = margin_ref.shape[0]

    @pl.when(pl.program_id(0) == 0)
    def _():
        high, low = split_bf16(margin_ref[...])
        turn[0:cols, :] = high
        turn[cols:, :] = low

    at = 0
    total = None
    for high_ref, low_ref in zip(halves[::2], halves[1::2]):
        upto = at + high_ref.shape[0]
        both = jnp.dot(turn[:, at:upto], high_ref[...], preferred_element_type=F32)
        low = jnp.dot(turn[0:cols, at:upto], low_ref[...], preferred_element_type=F32)
        value = both[0:cols] + both[cols:] + low
        total = value if total is None else total + value
        at = upto
    res[...] = total
    for s in range(out_ref.shape[0]):
        value = res[4 * s:4 * s + 4, :]
        out_ref[s] = bases[0][s] - value if bases else value


def rotated(margin, side, halves, *bases):
    cols, rows = margin.shape[0] // 2, margin.shape[1]
    width = halves[0].shape[1]
    out = jax.ShapeDtypeStruct((cols // 4, 4, width), F32)
    return pl.pallas_call(
        functools.partial(rotate_kernel, len(halves)),
        grid=(width // WIDE,),
        out_shape=out,
        in_specs=[pl.BlockSpec((cols, rows), lambda k: (side, 0))]
        + [chunk_spec(v, WIDE) for v in (*halves, *bases)],
        out_specs=chunk_spec(out, WIDE),
        scratch_shapes=[pltpu.VMEM((2 * cols, rows), BF16), pltpu.VMEM((cols, WIDE), F32)],
        cost_estimate=pl.CostEstimate(
            flops=6 * rows * cols * width, transcendentals=0,
            bytes_accessed=4 * (rows + 2 * cols) * width,
        ),
        compiler_params=pltpu.CompilerParams(vmem_limit_bytes=48 * 1024 * 1024),
        name="rotated",
    )(margin, *halves, *bases)


def shards(orbitals, potential, magic_taps, kinetic_taps):
    own = to_cols(orbitals)
    hpsi = hamiltonian(orbitals, potential, magic_taps, kinetic_taps)
    own, _ = lax.optimization_barrier((own, hpsi))
    left, right = step_x(own, 1), step_x(own, -1)
    hpsi_cols = to_cols(hpsi)
    half = NSPLIT // 2
    far_a, far_b = step_x(left[:half], 1), step_x(right[half:], -1)
    hpsi_swap = swap_core(hpsi_cols)
    near, *near_halves, hsp = near_part([own, left, right], hpsi_cols, hpsi_swap)
    part, *far_halves = far_part(near, hsp, [far_a, far_b])
    mine = jnp.sum(exchange(part.reshape(NSPLIT, -1, part.shape[1])), axis=0)
    margin = spread(spread(mine, ("zl", "zh"), 8), ("y",), 4)
    halves = near_halves + far_halves
    from_other = swap_core(rotated(margin, 1, halves))
    grad_cols = rotated(margin, 0, halves, hpsi_cols) - from_other
    back = exchange(grad_cols)
    return back.transpose(1, 0, 2).reshape(orbitals.shape)


def solution(mesh):
    fine = Mesh(mesh.devices.reshape(SPLIT), NAMES)
    placed = (P(NAMES, None), P(), P(), P())
    return jax.shard_map(
        shards, mesh=fine, in_specs=placed, out_specs=P(NAMES, None), check_vma=False
    )
```
